256 devices in a mesh: seq: 32 (over x, z), mlp: 8 (over y, core).
Axes of the slice: x: 4, y: 4, z: 8, core: 2. Of those that a mesh axis runs over, the one named last changes fastest.
Arguments:
- queries: bfloat16 [1024, 2560], P(('seq', 'mlp')), may hold values from -8 to 8
- new_kv: bfloat16 [1024, 512], P(('seq', 'mlp')), may hold values from -5 to 5
- kv_cache: bfloat16 [4352, 128, 512], P(('seq', 'mlp')), may hold values from -4 to 4, as said below
- lengths: int32 [256], replicated, may hold values from 256 to 16384, as said below
- page_table: int32 [256, 128], replicated, may hold values from -1 to 4351, as said below
- residual: bfloat16 [1024, 2560], P('seq', 'mlp'), may hold values from -3 to 3
- out_weight: bfloat16 [2560, 2560], P(None, 'mlp'), may hold values from -0.125 to 0.125
- norm_gain: float32 [2560], replicated, may hold values from 0.1 to 1.9
- gate_weight: bfloat16 [2560, 3840], P(None, 'mlp'), may hold values from -0.125 to 0.125
- up_weight: bfloat16 [2560, 3840], P(None, 'mlp'), may hold values from -0.125 to 0.125
- down_weight: bfloat16 [3840, 2560], P('mlp'), may hold values from -0.09375 to 0.09375
- next_gain: float32 [2560], replicated, may hold values from 0.1 to 1.9
- qkv_weight: bfloat16 [2560, 3072], P(None, 'mlp'), may hold values from -0.125 to 0.125
Outputs:
- attended: bfloat16 [1024, 2560], P(('seq', 'mlp'))
- residual_out: bfloat16 [1024, 2560], P('seq', 'mlp')
- next_qkv: bfloat16 [1024, 3072], P('seq', 'mlp')
The draws below stay inside these ranges and needn't reach their ends.
Inputs may be any that keep to these rules, and one draw needn't show every extreme that they name: `lengths`: lengths have a heavy tail; at least one request has exactly 16384. page_table[r, p] is a slot exactly for the pages p holding positions max(0, lengths[r] - 2047) to lengths[r] - 1, and -1 elsewhere. Slots d * 17 to d * 17 + 16 lie on device d of seq+mlp. All pages of request r lie in consecutive slots of ONE device, whose mlp index is r modulo 8; a device may hold the pages of several requests or of none. No slot holds two pages; some device of every mlp index has all 17 slots in use. `kv_cache`: unused slots hold arbitrary values.
All inputs are finite; a program needn't handle non-finite values.
Results may differ from the reference program's by a relative error of at most 0.011.
Values may be sent and summed in bfloat16 or wider, within the bound.
No kernel may reach another device: no remote copies, remote signals or barrier semaphores. Data moves between devices by JAX's collectives and lax.ppermute only.
A program may use at most 64 MiB of HBM per device.

```python
import jax
import jax.numpy as jnp
from jax import lax

D = 2560
HEADS = 10
HD = 256
FF = 3840
QKV = 3072
WINDOW = 2048
PAGE = 128
NEWTOK = 4
MAXLEN = 16384
MAXP = 128
SLOTS = 17
REQUESTS = 256
POOL = 4352
N_SEQ = 32
N_MLP = 8


def length_law(key):
    base = 2 * PAGE
    levels = (MAXLEN // base).bit_length()
    key_level, key_extra, key_pick = jax.random.split(key, 3)
    exponent = jax.random.randint(key_level, (REQUESTS,), 0, levels)
    spread = base * jnp.left_shift(jnp.int32(1), exponent)
    extra = jax.random.randint(key_extra, (REQUESTS,), 0, 1 << 30) % spread
    drawn = jnp.minimum(spread + extra, MAXLEN)
    full_seq = jax.random.randint(key_pick, (N_MLP,), 0, N_SEQ)
    rows = jnp.arange(REQUESTS)
    row_seq = rows // N_MLP
    row_col = rows % N_MLP
    full_row = row_seq == full_seq[row_col]
    drawn = jnp.where(full_row, MAXLEN - PAGE + 1, drawn)
    long_row = (full_seq[0] + 1) % N_SEQ * N_MLP
    return jnp.where(rows == long_row, MAXLEN, drawn).astype(jnp.int32)


def draw_lengths(key, part):
    return length_law(jax.random.fold_in(key, 11))


def column_table(column_key, column, col_first, col_count):
    key_order, key_holder = jax.random.split(column_key, 2)
    order = jax.random.permutation(key_order, N_SEQ).astype(jnp.int32)

    def place(carry, row):
        bin_now, fill = carry
        need = col_count[row]
        overflow = fill + need > SLOTS
        bin_next = jnp.where(overflow, bin_now + 1, bin_now)
        start = jnp.where(overflow, 0, fill)
        return ((bin_next, start + need), (bin_next, start))
    _, (bins, starts) = lax.scan(place, (jnp.int32(0), jnp.int32(0)), order)
    row_bin = jnp.zeros((N_SEQ,), jnp.int32).at[order].set(bins)
    row_start = jnp.zeros((N_SEQ,), jnp.int32).at[order].set(starts)
    holder = jax.random.permutation(key_holder, N_SEQ).astype(jnp.int32)[row_bin]
    page_ids = jnp.arange(MAXP, dtype=jnp.int32)[None, :]
    relative = page_ids - col_first[:, None]
    inside = (relative >= 0) & (relative < col_count[:, None])
    slot = (holder * N_MLP + column)[:, None] * SLOTS + row_start[:, None] + relative
    return jnp.where(inside, slot, -1)


def draw_page_table(key, part):
    lengths = length_law(jax.random.fold_in(key, 11))
    lowest = jnp.maximum(0, lengths - WINDOW + 1)
    first_page = lowest // PAGE
    page_total = (lengths - 1) // PAGE - first_page + 1
    grouped_first = first_page.reshape(N_SEQ, N_MLP).transpose(1, 0)
    grouped_count = page_total.reshape(N_SEQ, N_MLP).transpose(1, 0)
    base_key = jax.random.fold_in(key, 23)
    column_keys = jax.vmap(lambda column: jax.random.fold_in(base_key, column))(jnp.arange(N_MLP))
    tables = jax.vmap(column_table)(column_keys, jnp.arange(N_MLP, dtype=jnp.int32), grouped_first, grouped_count)
    return tables.transpose(1, 0, 2).reshape(REQUESTS, MAXP).astype(jnp.int32)


def draw_queries(key, part):
    key_main = jax.random.fold_in(jax.random.fold_in(key, 5), 0)
    shape = (REQUESTS * NEWTOK, HEADS, HD)
    entries = jnp.clip(2.5 * jax.random.normal(key_main, shape, jnp.float32), -8.0, 8.0)
    return entries.reshape(REQUESTS * NEWTOK, HEADS * HD).astype(jnp.bfloat16)


def draw_kv_cache(key, part):
    key_main = jax.random.fold_in(jax.random.fold_in(key, 9), 0)
    shape = (POOL, PAGE, 2 * HD)
    values = jnp.clip(jax.random.normal(key_main, shape, jnp.float32), -4.0, 4.0)
    return values.astype(jnp.bfloat16)


def shard_levels(key, extent, cuts, least, largest):
    level = 1.0
    for dim, blocks in cuts:
        heights = jax.random.uniform(jax.random.fold_in(jax.random.fold_in(key, 6), dim), (blocks,), jnp.float32, least / len(cuts), largest / len(cuts))
        level = level * jnp.repeat(jnp.exp(heights), extent[dim] // blocks).reshape((-1,) + (1,) * (len(extent) - 1 - dim))
    return level


def normal_values(key, dims, scale, limit, cuts=(), held_as=jnp.bfloat16):
    level = shard_levels(key, dims, cuts, -0.22, 0.18) if cuts else 1.0
    result = jax.random.normal(key, dims, jnp.float32) * scale * level
    return jnp.minimum(jnp.maximum(result, -limit), limit).astype(held_as)


def setup_inputs(seed: int = 0) -> dict:
    key_of = jax.random.split(jax.random.key(seed), 14)
    queries = draw_queries(jax.random.fold_in(key_of[13], 71), 0)
    new_kv = normal_values(key_of[1], (REQUESTS * NEWTOK, 2 * HD), 1.0, 5.0, ((0, 256),))
    kv_cache = draw_kv_cache(jax.random.fold_in(key_of[13], 71), 0)
    lengths = draw_lengths(jax.random.fold_in(key_of[13], 71), 0)
    page_table = draw_page_table(jax.random.fold_in(key_of[13], 71), 0)
    residual = normal_values(key_of[5], (REQUESTS * NEWTOK, D), 0.5, 3.0, ((0, 32), (1, 8)))
    out_weight = normal_values(key_of[6], (D, D), D ** -0.5, 0.125, ((1, 8),))
    norm_gain = jnp.clip(1.0 + 0.18 * jax.random.normal(key_of[7], (D,), jnp.float32), 0.1, 1.9)
    gate_weight = normal_values(key_of[8], (D, FF), D ** -0.5, 0.125, ((1, 8),))
    up_weight = normal_values(key_of[9], (D, FF), D ** -0.5, 0.125, ((1, 8),))
    down_weight = normal_values(key_of[10], (FF, D), FF ** -0.5, 0.09375, ((0, 8),))
    next_gain = jnp.clip(1.0 + 0.18 * jax.random.normal(key_of[11], (D,), jnp.float32), 0.1, 1.9)
    qkv_weight = normal_values(key_of[12], (D, QKV), D ** -0.5, 0.125, ((1, 8),))
    return {"queries": queries, "new_kv": new_kv, "kv_cache": kv_cache, "lengths": lengths, "page_table": page_table, "residual": residual, "out_weight": out_weight, "norm_gain": norm_gain, "gate_weight": gate_weight, "up_weight": up_weight, "down_weight": down_weight, "next_gain": next_gain, "qkv_weight": qkv_weight}


NEG_FILL = -1e+30

def block_partial(query_rows, key_rows, value_rows, valid_mask):
    scores = jnp.einsum('qhd,kd->qhk', query_rows.astype(jnp.float32), key_rows.astype(jnp.float32)) * HD ** (-0.5)
    mask_full = valid_mask[:, None, :]
    block_max = lax.optimization_barrier(jnp.max(jnp.where(mask_full, scores, NEG_FILL), axis=-1))
    weights = jnp.where(mask_full, jnp.exp(scores - block_max[..., None]), 0.0)
    block_sum = lax.optimization_barrier(jnp.sum(weights, axis=-1))
    block_acc = jnp.einsum('qhk,kd->qhd', weights.astype(jnp.bfloat16).astype(jnp.float32), value_rows.astype(jnp.float32))
    return (block_max, block_sum, block_acc)

def rms_norm(values, gain):
    floats = values.astype(jnp.float32)
    scaled = floats * lax.rsqrt(lax.optimization_barrier(jnp.mean(floats * floats, axis=-1, keepdims=True)) + 1e-06)
    return (scaled * gain).astype(jnp.bfloat16)

def reference(queries, new_kv, kv_cache, lengths, page_table, residual, out_weight, norm_gain, gate_weight, up_weight, down_weight, next_gain, qkv_weight):
    query_grid = queries.reshape(REQUESTS, NEWTOK, HEADS, HD)
    new_grid = new_kv.reshape(REQUESTS, NEWTOK, 2 * HD)
    offsets = jnp.arange(NEWTOK, dtype=jnp.int32)
    page_pos = jnp.arange(MAXP, dtype=jnp.int32)[:, None] * PAGE + jnp.arange(PAGE, dtype=jnp.int32)[None, :]

    def one_request(request):
        length = lengths[request]
        slot_ids = page_table[request]
        used = slot_ids >= 0
        pages = kv_cache[jnp.maximum(slot_ids, 0)]
        valid = used[:, None, None] & (page_pos[:, None, :] < length) & (page_pos[:, None, :] >= length + offsets[None, :, None] - (WINDOW - 1))
        own_query = query_grid[request]

        def page_term(page_rows, page_valid):
            return block_partial(own_query, page_rows[:, :HD], page_rows[:, HD:], page_valid)
        maxima, sums, accums = jax.vmap(page_term)(pages, valid)
        causal = offsets[:, None] >= offsets[None, :]
        new_max, new_sum, new_acc = block_partial(own_query, new_grid[request][:, :HD], new_grid[request][:, HD:], causal)
        maxima = jnp.concatenate([maxima, new_max[None]], axis=0)
        sums = jnp.concatenate([sums, new_sum[None]], axis=0)
        accums = jnp.concatenate([accums, new_acc[None]], axis=0)
        peak = lax.optimization_barrier(jnp.max(maxima, axis=0))
        factor = jnp.exp(maxima - peak[None])
        total = lax.optimization_barrier(jnp.sum(factor * sums, axis=0))
        accum = lax.optimization_barrier(jnp.sum(factor[..., None] * accums, axis=0))
        return (accum / total[..., None]).reshape(NEWTOK, HEADS * HD).astype(jnp.bfloat16)
    attended = lax.map(one_request, jnp.arange(REQUESTS, dtype=jnp.int32)).reshape(REQUESTS * NEWTOK, D)
    stream = (residual.astype(jnp.float32) + jnp.dot(attended, out_weight, preferred_element_type=jnp.float32)).astype(jnp.bfloat16)
    normed = rms_norm(stream, norm_gain)
    gate = jnp.dot(normed, gate_weight, preferred_element_type=jnp.float32)
    upward = jnp.dot(normed, up_weight, preferred_element_type=jnp.float32)
    hidden = (jax.nn.gelu(gate, approximate=True) * upward).astype(jnp.bfloat16)
    residual_out = (stream.astype(jnp.float32) + jnp.dot(hidden, down_weight, preferred_element_type=jnp.float32)).astype(jnp.bfloat16)
    normed_next = rms_norm(residual_out, next_gain)
    next_qkv = jnp.dot(normed_next, qkv_weight, preferred_element_type=jnp.float32).astype(jnp.bfloat16)
    return (attended, residual_out, next_qkv)
```

```python
import jax
import jax.numpy as jnp
from jax import lax
from jax.experimental import pallas as pl
from jax.experimental.pallas import tpu as pltpu
from jax.sharding import PartitionSpec as P

WINDOW = 2048
NEG_FILL = -1e30


def attend_pages(code_ref, length_ref, rows_ref, cache_ref, out_ref, max_ref, sum_ref, acc_ref):
    slot_count, page_len, kv_width = cache_ref.shape
    head_dim = kv_width // 2
    token_count = out_ref.shape[1]
    query_rows = out_ref.shape[2] // head_dim * token_count
    page_count = 128
    scale = head_dim ** (-0.5)
    token = lax.broadcasted_iota(jnp.int32, (query_rows, page_len), 0) % token_count
    lane = lax.broadcasted_iota(jnp.int32, (query_rows, page_len), 1)
    contract_last = (((1,), (1,)), ((), ()))
    for slot in range(slot_count):
        code = code_ref[slot]
        entry = jnp.maximum(code - 1, 0)
        source = entry // page_count
        page = entry % page_count
        length = jnp.where(code > 0, length_ref[source], 0)
        query = rows_ref[source, :query_rows, :]
        scores = (
            lax.dot_general(
                query, cache_ref[slot, :, :head_dim], contract_last, preferred_element_type=jnp.float32
            )
            * scale
        )
        position = page * page_len + lane
        valid = (position < length) & (position >= length + token - (WINDOW - 1))
        peak = jnp.max(jnp.where(valid, scores, NEG_FILL), axis=1, keepdims=True)
        weights = jnp.where(valid, jnp.exp(scores - peak), 0.0)
        max_ref[slot] = jnp.broadcast_to(peak, (query_rows, 128))
        sum_ref[slot] = jnp.broadcast_to(jnp.sum(weights, axis=1, keepdims=True), (query_rows, 128))
        acc_ref[slot] = jnp.dot(
            weights.astype(jnp.bfloat16),
            cache_ref[slot, :, head_dim:],
            preferred_element_type=jnp.float32,
        )
    last = slot_count
    for slot in range(slot_count):
        code = code_ref[slot]
        entry = jnp.maximum(code - 1, 0)
        source = entry // page_count
        before = code_ref[max(slot - 1, 0)]
        after = code_ref[min(slot + 1, slot_count - 1)]
        same_before = (before > 0) & ((before - 1) // page_count == source) & (slot > 0)
        same_after = (after > 0) & ((after - 1) // page_count == source) & (slot < slot_count - 1)
        used = code > 0

        @pl.when(used & jnp.logical_not(same_before))
        def _():
            query = rows_ref[source, :query_rows, :]
            fresh = rows_ref[source, query_rows:, :]
            scores = (
                lax.dot_general(query, fresh, contract_last, preferred_element_type=jnp.float32) * scale
            )
            row_token = lax.broadcasted_iota(jnp.int32, scores.shape, 0) % token_count
            column = lax.broadcasted_iota(jnp.int32, scores.shape, 1)
            valid = column <= row_token
            peak = jnp.max(jnp.where(valid, scores, NEG_FILL), axis=1, keepdims=True)
            weights = jnp.where(valid, jnp.exp(scores - peak), 0.0)
            total = jnp.sum(weights, axis=1, keepdims=True)
            rounded = weights.astype(jnp.bfloat16).astype(jnp.float32)
            acc = jnp.zeros((query_rows, head_dim), jnp.float32)
            for new in range(token_count):
                value = fresh[token_count + new : token_count + new + 1, :].astype(jnp.float32)
                acc = acc + rounded[:, new : new + 1] * value
            max_ref[last] = jnp.broadcast_to(peak, (query_rows, 128))
            sum_ref[last] = jnp.broadcast_to(total, (query_rows, 128))
            acc_ref[last] = acc

        @pl.when(used)
        def _():
            old_max = max_ref[last]
            page_max = max_ref[slot]
            peak = jnp.maximum(old_max, page_max)
            old_factor = jnp.exp(old_max - peak)
            page_factor = jnp.exp(page_max - peak)
            max_ref[last] = peak
            sum_ref[last] = sum_ref[last] * old_factor + sum_ref[slot] * page_factor
            acc_ref[last] = acc_ref[last] * jnp.concatenate([old_factor, old_factor], axis=1) + acc_ref[
                slot
            ] * jnp.concatenate([page_factor, page_factor], axis=1)

        @pl.when(used & jnp.logical_not(same_after))
        def _():
            total = sum_ref[last]
            result = acc_ref[last] / jnp.concatenate([total, total], axis=1)
            for head in range(query_rows // token_count):
                out_ref[source, :, head * head_dim : (head + 1) * head_dim] = result[
                    head * token_count : (head + 1) * token_count, :
                ].astype(jnp.bfloat16)


def feed_forward(stream_ref, gain_ref, gate_ref, up_ref, down_ref, keep_ref, send_ref, core_ref=None):
    parts, rows, width = stream_ref.shape
    square = jnp.zeros((rows, 1), jnp.float32)
    for part in range(parts):
        floats = stream_ref[part].astype(jnp.float32)
        square = square + jnp.sum(floats * floats, axis=1, keepdims=True)
    factor = lax.rsqrt(square / (parts * width) + 1e-06)
    gate = jnp.zeros((rows, gate_ref.shape[2]), jnp.float32)
    upward = jnp.zeros((rows, up_ref.shape[2]), jnp.float32)
    for part in range(parts):
        normed = (stream_ref[part].astype(jnp.float32) * factor * gain_ref[part]).astype(jnp.bfloat16)
        gate = gate + jnp.dot(normed, gate_ref[part], preferred_element_type=jnp.float32)
        upward = upward + jnp.dot(normed, up_ref[part], preferred_element_type=jnp.float32)
    hidden = (jax.nn.gelu(gate, approximate=True) * upward).astype(jnp.bfloat16)
    partial = jnp.dot(hidden, down_ref[...], preferred_element_type=jnp.float32)
    half = partial.shape[1] // 2
    keep_ref[...] = partial[:, :half]
    send_ref[...] = partial[:, half:]


def rms_norm(values, gain):
    floats = values.astype(jnp.float32)
    scaled = floats * lax.rsqrt(jnp.mean(floats * floats, axis=-1, keepdims=True) + 1e-06)
    return (scaled * gain).astype(jnp.bfloat16)


def spread(block, axis):
    copies = jnp.broadcast_to(block[None], (lax.axis_size(axis),) + block.shape)
    return lax.all_to_all(copies, axis, split_axis=0, concat_axis=0, tiled=True)


def shards(
    queries,
    new_kv,
    kv_cache,
    lengths,
    page_table,
    residual,
    out_weight,
    norm_gain,
    gate_weight,
    up_weight,
    down_weight,
    next_gain,
    qkv_weight,
):
    seq_count = lax.axis_size("seq")
    mlp_count = lax.axis_size("mlp")
    seq_place = lax.axis_index("seq")
    mlp_place = lax.axis_index("mlp")
    device = seq_place * mlp_count + mlp_place
    slot_count, page_len, kv_width = kv_cache.shape
    head_dim = kv_width // 2
    token_count, width = queries.shape
    head_count = width // head_dim
    page_count = page_table.shape[1]
    bf16 = jnp.bfloat16

    own_rows = jnp.concatenate(
        [
            queries.reshape(token_count, head_count, head_dim).transpose(1, 0, 2).reshape(-1, head_dim),
            new_kv[:, :head_dim],
            new_kv[:, head_dim:],
        ],
        axis=0,
    )
    column_rows = spread(own_rows, "seq")

    column_table = lax.dynamic_index_in_dim(
        page_table.reshape(seq_count, mlp_count, page_count), mlp_place, 1, keepdims=False
    )
    column_lengths = lax.dynamic_index_in_dim(
        lengths.reshape(seq_count, mlp_count), mlp_place, 1, keepdims=False
    )
    entry = (
        jnp.arange(seq_count, dtype=jnp.int32)[:, None] * page_count
        + jnp.arange(page_count, dtype=jnp.int32)[None, :]
        + 1
    )
    slots = device * slot_count + jnp.arange(slot_count, dtype=jnp.int32)
    codes = jnp.max(
        jnp.where(column_table[None] == slots[:, None, None], entry[None], 0), axis=(1, 2)
    )
    own_table = lax.dynamic_index_in_dim(column_table, seq_place, 0, keepdims=False)
    holder = jnp.max(own_table) // (slot_count * mlp_count)

    smem = pl.BlockSpec(memory_space=pltpu.SMEM)
    vmem = pl.BlockSpec(memory_space=pltpu.VMEM)
    query_rows = token_count * head_count
    held = pl.pallas_call(
        attend_pages,
        out_shape=jax.ShapeDtypeStruct((seq_count, token_count, width), bf16),
        in_specs=[smem, smem, vmem, vmem],
        out_specs=vmem,
        scratch_shapes=[
            pltpu.VMEM((slot_count + 1, query_rows, 128), jnp.float32),
            pltpu.VMEM((slot_count + 1, query_rows, 128), jnp.float32),
            pltpu.VMEM((slot_count + 1, query_rows, head_dim), jnp.float32),
        ],
        name="attend_pages",
    )(codes, column_lengths, column_rows, kv_cache)
    returned = lax.all_to_all(held, "seq", split_axis=0, concat_axis=0, tiled=True)
    attended = lax.dynamic_index_in_dim(returned, holder, 0, keepdims=False)

    rows = spread(attended, "mlp").reshape(mlp_count * token_count, width)
    attention_out = jnp.dot(rows, out_weight, preferred_element_type=jnp.float32)
    stream = (residual.astype(jnp.float32) + attention_out).astype(bf16)
    streams = spread(stream, "mlp")

    row_count, part_width = stream.shape
    hidden_count = gate_weight.shape[1]
    half = width // 2
    low, high = pl.pallas_call(
        feed_forward,
        out_shape=[jax.ShapeDtypeStruct((row_count, half), jnp.float32)] * 2,
        in_specs=[vmem] * 5,
        out_specs=[vmem] * 2,
        name="feed_forward",
    )(
        streams,
        norm_gain.reshape(mlp_count, 1, part_width),
        gate_weight.reshape(mlp_count, part_width, hidden_count),
        up_weight.reshape(mlp_count, part_width, hidden_count),
        down_weight,
    )
    is_high = mlp_place % 2 == 1
    keep = jnp.where(is_high, high, low)
    send = jnp.where(is_high, low, high).astype(bf16)
    pair = [(i, i ^ 1) for i in range(mlp_count)]
    chip_half = keep + lax.ppermute(send, "mlp", pair).astype(jnp.float32)
    chip_send = chip_half.astype(bf16)
    total_half = chip_half
    for shift in (2, 6, 4):
        got = lax.ppermute(chip_send, "mlp", [(i, (i + shift) % mlp_count) for i in range(mlp_count)])
        total_half = total_half + got.astype(jnp.float32)
    whole_stream = streams.transpose(1, 0, 2).reshape(row_count, width)
    stream_half = jnp.where(is_high, whole_stream[:, half:], whole_stream[:, :half])
    after_half = (stream_half.astype(jnp.float32) + total_half).astype(bf16)
    other_half = lax.ppermute(after_half, "mlp", pair)
    full_after = jnp.concatenate(
        [jnp.where(is_high, other_half, after_half), jnp.where(is_high, after_half, other_half)], axis=1
    )
    shard_after = lax.dynamic_slice_in_dim(full_after, mlp_place * part_width, part_width, 1)
    normed_next = rms_norm(full_after, next_gain)
    next_qkv = jnp.dot(normed_next, qkv_weight, preferred_element_type=jnp.float32).astype(bf16)
    return (attended, shard_after, next_qkv)


def solution(mesh):
    return jax.shard_map(
        shards,
        mesh=mesh,
        in_specs=(
            P(("seq", "mlp"), None),
            P(("seq", "mlp"), None),
            P(("seq", "mlp"), None, None),
            P(),
            P(),
            P("seq", "mlp"),
            P(None, "mlp"),
            P(),
            P(None, "mlp"),
            P(None, "mlp"),
            P("mlp", None),
            P(),
            P(None, "mlp"),
        ),
        out_specs=(P(("seq", "mlp"), None), P("seq", "mlp"), P("seq", "mlp")),
        check_vma=False,
    )
```

```python
import jax
import jax.numpy as jnp
from jax import lax
from jax.experimental import pallas as pl
from jax.experimental.pallas import tpu as pltpu
from jax.sharding import PartitionSpec as P

WINDOW = 2048
NEG_FILL = -1e30
LAST = (((1,), (1,)), ((), ()))
F32 = jnp.float32
BF16 = jnp.bfloat16


def head_major(values, head_dim):
    width = values.shape[1]
    return jnp.concatenate(
        [values[:, start : start + head_dim] for start in range(0, width, head_dim)], axis=0
    )


def put_heads(column, token_count, lanes):
    lane = lax.broadcasted_iota(jnp.int32, (token_count, lanes), 1)
    placed = jnp.zeros((token_count, lanes), F32)
    for head in range(column.shape[0] // token_count):
        part = column[head * token_count : (head + 1) * token_count, :]
        placed = jnp.where(lane == head, part, placed)
    return placed


def send_queries(queries_ref, out_ref):
    rows = head_major(queries_ref[...].astype(F32), out_ref.shape[2]).astype(BF16)
    for place in range(out_ref.shape[0]):
        out_ref[place] = rows


def attend_new(queries_ref, new_ref, max_ref, sum_ref, acc_ref):
    token_count, width = queries_ref.shape
    head_dim = new_ref.shape[1] // 2
    query = head_major(queries_ref[...].astype(F32), head_dim).astype(BF16)
    scores = lax.dot_general(
        query, new_ref[:, :head_dim], LAST, preferred_element_type=F32
    ) * head_dim ** (-0.5)
    token = lax.broadcasted_iota(jnp.int32, scores.shape, 0) % token_count
    column = lax.broadcasted_iota(jnp.int32, scores.shape, 1)
    valid = column <= token
    peak = jnp.max(jnp.where(valid, scores, NEG_FILL), axis=1, keepdims=True)
    weights = jnp.where(valid, jnp.exp(scores - peak), 0.0)
    rounded = weights.astype(BF16).astype(F32)
    values = new_ref[:, head_dim:].astype(F32)
    acc = jnp.zeros((query.shape[0], head_dim), F32)
    for new in range(token_count):
        acc = acc + rounded[:, new : new + 1] * values[new : new + 1, :]
    max_ref[...] = put_heads(peak, token_count, max_ref.shape[1])
    sum_ref[...] = put_heads(jnp.sum(weights, axis=1, keepdims=True), token_count, sum_ref.shape[1])
    for head in range(width // head_dim):
        acc_ref[:, head * head_dim : (head + 1) * head_dim] = acc[
            head * token_count : (head + 1) * token_count, :
        ]


def attend_pages(
    code_ref, length_ref, rows_ref, far_ref, out_ref, max_ref, sum_ref, acc_ref, cache_ref, copied
):
    slot_count, page_len, kv_width = cache_ref.shape
    head_dim = kv_width // 2
    token_count = out_ref.shape[1]
    width = out_ref.shape[2] - 128
    query_rows = rows_ref.shape[1]
    head_count = width // head_dim
    page_count = 128
    scale = head_dim ** (-0.5)
    copies = [
        pltpu.make_async_copy(far_ref.at[slot], cache_ref.at[slot], copied.at[slot])
        for slot in range(slot_count)
    ]
    for copy in copies:
        copy.start()
    token = lax.broadcasted_iota(jnp.int32, (query_rows, page_len), 0) % token_count
    lane = lax.broadcasted_iota(jnp.int32, (query_rows, page_len), 1)
    for slot in range(slot_count):
        code = code_ref[slot]
        entry = jnp.maximum(code - 1, 0)
        source = entry // page_count
        page = entry % page_count
        length = jnp.where(code > 0, length_ref[source], 0)
        copies[slot].wait()
        scores = (
            lax.dot_general(
                rows_ref[source], cache_ref[slot, :, :head_dim], LAST, preferred_element_type=F32
            )
            * scale
        )
        position = page * page_len + lane
        valid = (position < length) & (position >= length + token - (WINDOW - 1))
        peak = jnp.max(jnp.where(valid, scores, NEG_FILL), axis=1, keepdims=True)
        weights = jnp.where(valid, jnp.exp(scores - peak), 0.0)
        max_ref[slot] = jnp.broadcast_to(peak, (query_rows, 128))
        sum_ref[slot] = jnp.broadcast_to(jnp.sum(weights, axis=1, keepdims=True), (query_rows, 128))
        acc_ref[slot] = jnp.dot(
            weights.astype(BF16), cache_ref[slot, :, head_dim:], preferred_element_type=F32
        )
    last = slot_count
    for slot in range(slot_count):
        code = code_ref[slot]
        source = jnp.maximum(code - 1, 0) // page_count
        before = code_ref[max(slot - 1, 0)]
        after = code_ref[min(slot + 1, slot_count - 1)]
        same_before = (before > 0) & ((before - 1) // page_count == source) & (slot > 0)
        same_after = (after > 0) & ((after - 1) // page_count == source) & (slot < slot_count - 1)
        used = code > 0

        @pl.when(used & jnp.logical_not(same_before))
        def _():
            max_ref[last] = max_ref[slot]
            sum_ref[last] = sum_ref[slot]
            acc_ref[last] = acc_ref[slot]

        @pl.when(used & same_before)
        def _():
            old_max = max_ref[last]
            page_max = max_ref[slot]
            peak = jnp.maximum(old_max, page_max)
            old_factor = jnp.exp(old_max - peak)
            page_factor = jnp.exp(page_max - peak)
            max_ref[last] = peak
            sum_ref[last] = sum_ref[last] * old_factor + sum_ref[slot] * page_factor
            acc_ref[last] = acc_ref[last] * jnp.concatenate([old_factor, old_factor], axis=1) + acc_ref[
                slot
            ] * jnp.concatenate([page_factor, page_factor], axis=1)

        @pl.when(used & jnp.logical_not(same_after))
        def _():
            total = sum_ref[last]
            result = acc_ref[last] / jnp.concatenate([total, total], axis=1)
            for head in range(head_count):
                out_ref[source, :, head * head_dim : (head + 1) * head_dim] = result[
                    head * token_count : (head + 1) * token_count, :
                ].astype(BF16)
            whole = put_heads((max_ref[last] + jnp.log(total))[:, :1], token_count, 128)
            high = whole.astype(BF16).astype(F32)
            middle = (whole - high).astype(BF16).astype(F32)
            low = whole - high - middle
            lanes = lax.broadcasted_iota(jnp.int32, whole.shape, 1)
            packed = jnp.where(
                lanes < 16,
                high,
                jnp.where(lanes < 32, pltpu.roll(middle, 16, 1), pltpu.roll(low, 32, 1)),
            )
            out_ref[source, :, width:] = packed.astype(BF16)


def merge_new(holder_ref, got_ref, max_ref, sum_ref, acc_ref, attended_ref, spread_ref):
    token_count, width = attended_ref.shape
    holder = holder_ref[0]
    packed = got_ref[holder, :, width:].astype(F32)
    cached = packed + pltpu.roll(packed, 128 - 16, 1) + pltpu.roll(packed, 128 - 32, 1)
    new_max = max_ref[...]
    peak = jnp.maximum(cached, new_max)
    cached_factor = jnp.exp(cached - peak)
    new_factor = jnp.exp(new_max - peak)
    inverse = 1.0 / (cached_factor + new_factor * sum_ref[...])
    cached_factor = cached_factor * inverse
    new_factor = new_factor * inverse
    head_dim = 256
    for head in range(width // head_dim):
        span = slice(head * head_dim, (head + 1) * head_dim)
        rows = (
            got_ref[holder, :, span].astype(F32) * cached_factor[:, head : head + 1]
            + acc_ref[:, span] * new_factor[:, head : head + 1]
        ).astype(BF16)
        attended_ref[:, span] = rows
        for place in range(spread_ref.shape[0]):
            spread_ref[place, :, span] = rows


def project_out(rows_ref, weight_ref, residual_ref, out_ref):
    places, token_count, width = rows_ref.shape
    rows = jnp.concatenate([rows_ref[place].astype(F32) for place in range(places)], axis=0).astype(BF16)
    attention_out = lax.dot_general(rows, weight_ref[...], LAST, preferred_element_type=F32)
    stream = (residual_ref[...].astype(F32) + attention_out).astype(BF16)
    for place in range(places):
        out_ref[place] = stream


def feed_forward(
    core_ref,
    stream_ref,
    gain_ref,
    gate_far,
    up_far,
    down_far,
    keep_ref,
    send_ref,
    stream_half_ref,
    whole_ref,
    halves_ref,
    gate_ref,
    up_ref,
    down_ref,
    copied,
):
    parts, rows, width = stream_ref.shape
    total = parts * width
    half = total // 2
    chunks = copied.shape[0] // 3
    step = gate_ref.shape[0] // chunks
    copies = []
    for chunk in range(chunks):
        span = pl.ds(chunk * step, step)
        for far, near_ref in ((gate_far, gate_ref), (up_far, up_ref), (down_far, down_ref)):
            copies.append(pltpu.make_async_copy(far.at[span], near_ref.at[span], copied.at[len(copies)]))
            copies[-1].start()
    for part in range(parts):
        whole_ref[:, part * width : (part + 1) * width] = stream_ref[part].astype(F32)
    whole = whole_ref[...]
    square = jnp.sum(whole * whole, axis=1, keepdims=True)
    normed = (whole * lax.rsqrt(square / total + 1e-06) * gain_ref[...]).astype(BF16)
    core = core_ref[0]

    @pl.when(core == 0)
    def _():
        stream_half_ref[...] = whole_ref[:, :half]

    @pl.when(core == 1)
    def _():
        stream_half_ref[...] = whole_ref[:, half:]

    partial = jnp.zeros((rows, total), F32)
    for chunk in range(chunks):
        span = slice(chunk * step, (chunk + 1) * step)
        copies[3 * chunk].wait()
        gate = lax.dot_general(normed, gate_ref[span, :], LAST, preferred_element_type=F32)
        copies[3 * chunk + 1].wait()
        upward = lax.dot_general(normed, up_ref[span, :], LAST, preferred_element_type=F32)
        hidden = (jax.nn.gelu(gate, approximate=True) * upward).astype(BF16)
        copies[3 * chunk + 2].wait()
        partial = partial + jnp.dot(hidden, down_ref[span, :], preferred_element_type=F32)
    halves_ref[0] = partial[:, :half]
    halves_ref[1] = partial[:, half:]
    keep_ref[...] = halves_ref[core]
    send_ref[...] = halves_ref[1 - core].astype(BF16)


def add_pair(keep_ref, got_ref, send_ref):
    send_ref[...] = (keep_ref[...] + got_ref[...].astype(F32)).astype(BF16)


def add_chips(keep_ref, got_ref, first_ref, second_ref, third_ref, stream_ref, out_ref):
    total = keep_ref[...] + got_ref[...].astype(F32)
    total = total + first_ref[...].astype(F32) + second_ref[...].astype(F32) + third_ref[...].astype(F32)
    out_ref[...] = (stream_ref[...] + total).astype(BF16)


def project_next(place_ref, own_ref, other_ref, gain_ref, weight_ref, shard_ref, out_ref, whole_ref):
    rows, half = own_ref.shape
    core = place_ref[0] % 2

    @pl.when(core == 0)
    def _():
        whole_ref[:, :half] = own_ref[...].astype(F32)
        whole_ref[:, half:] = other_ref[...].astype(F32)

    @pl.when(core == 1)
    def _():
        whole_ref[:, half:] = own_ref[...].astype(F32)
        whole_ref[:, :half] = other_ref[...].astype(F32)

    part = shard_ref.shape[1]
    for place in range(2 * half // part):

        @pl.when(place_ref[0] == place)
        def _():
            shard_ref[...] = whole_ref[:, place * part : (place + 1) * part].astype(BF16)

    whole = whole_ref[...]
    square = jnp.sum(whole * whole, axis=1, keepdims=True)
    normed = (whole * lax.rsqrt(square / (2 * half) + 1e-06) * gain_ref[...]).astype(BF16)
    out_ref[...] = jnp.dot(normed, weight_ref[...], preferred_element_type=F32).astype(BF16)


SMEM = pl.BlockSpec(memory_space=pltpu.SMEM)
VMEM = pl.BlockSpec(memory_space=pltpu.VMEM)
FAR = pl.BlockSpec(memory_space=pl.ANY)


def near(array):
    return pltpu.with_memory_space_constraint(array, pltpu.VMEM)


def call(body, outs, scalars, arrays, far=(), scratch=(), copies=0):
    scratch_shapes = [pltpu.VMEM(shape, dtype) for shape, dtype in scratch]
    if copies:
        scratch_shapes.append(pltpu.SemaphoreType.DMA((copies,)))
    return pl.pallas_call(
        body,
        out_shape=[
            pltpu.VMEM(shape, dtype) if stays else jax.ShapeDtypeStruct(shape, dtype)
            for shape, dtype, stays in outs
        ],
        in_specs=[SMEM] * len(scalars) + [VMEM] * len(arrays) + [FAR] * len(far),
        out_specs=[VMEM] * len(outs),
        scratch_shapes=scratch_shapes,
        name=body.__name__,
    )(*scalars, *[near(array) for array in arrays], *far)


def exchange(copies, axis):
    return lax.all_to_all(copies, axis, split_axis=0, concat_axis=0, tiled=True)


def shards(
    queries,
    new_kv,
    kv_cache,
    lengths,
    page_table,
    residual,
    out_weight,
    norm_gain,
    gate_weight,
    up_weight,
    down_weight,
    next_gain,
    qkv_weight,
):
    seq_count = lax.axis_size("seq")
    mlp_count = lax.axis_size("mlp")
    seq_place = lax.axis_index("seq")
    mlp_place = lax.axis_index("mlp")
    device = seq_place * mlp_count + mlp_place
    slot_count, page_len, kv_width = kv_cache.shape
    head_dim = kv_width // 2
    token_count, width = queries.shape
    query_rows = token_count * (width // head_dim)
    page_count = page_table.shape[1]
    row_count, part_width = residual.shape
    half = width // 2

    (sent,) = call(send_queries, [((seq_count, query_rows, head_dim), BF16, True)], [], [queries])
    column_rows = exchange(sent, "seq")

    column_table = lax.dynamic_index_in_dim(
        page_table.reshape(seq_count, mlp_count, page_count), mlp_place, 1, keepdims=False
    )
    column_lengths = lax.dynamic_index_in_dim(
        lengths.reshape(seq_count, mlp_count), mlp_place, 1, keepdims=False
    )
    entry = (
        jnp.arange(seq_count, dtype=jnp.int32)[:, None] * page_count
        + jnp.arange(page_count, dtype=jnp.int32)[None, :]
        + 1
    )
    slots = device * slot_count + jnp.arange(slot_count, dtype=jnp.int32)
    codes = jnp.max(
        jnp.where(column_table[None] == slots[:, None, None], entry[None], 0), axis=(1, 2)
    )
    own_table = lax.dynamic_index_in_dim(column_table, seq_place, 0, keepdims=False)
    holder = (jnp.max(own_table) // (slot_count * mlp_count)).reshape(1)

    new_max, new_sum, new_acc = call(
        attend_new,
        [((token_count, 128), F32, True)] * 2 + [((token_count, width), F32, True)],
        [],
        [queries, new_kv],
    )
    (held,) = call(
        attend_pages,
        [((seq_count, token_count, width + 128), BF16, True)],
        [codes, column_lengths],
        [column_rows],
        [kv_cache],
        [
            ((slot_count + 1, query_rows, 128), F32),
            ((slot_count + 1, query_rows, 128), F32),
            ((slot_count + 1, query_rows, head_dim), F32),
            (kv_cache.shape, BF16),
        ],
        slot_count,
    )
    returned = exchange(held, "seq")
    attended, spread = call(
        merge_new,
        [((token_count, width), BF16, False), ((mlp_count, token_count, width), BF16, True)],
        [holder],
        [returned, new_max, new_sum, new_acc],
    )
    rows = exchange(spread, "mlp")
    (streams,) = call(
        project_out,
        [((mlp_count, row_count, part_width), BF16, True)],
        [],
        [rows, out_weight.T, residual],
    )
    streams = exchange(streams, "mlp")

    core = (mlp_place % 2).astype(jnp.int32).reshape(1)
    keep, send, stream_half = call(
        feed_forward,
        [((row_count, half), F32, True), ((row_count, half), BF16, True), ((row_count, half), F32, True)],
        [core],
        [streams, norm_gain.reshape(1, width)],
        [gate_weight.T, up_weight.T, down_weight],
        [
            ((row_count, width), F32),
            ((2, row_count, half), F32),
            (gate_weight.shape[::-1], BF16),
            (up_weight.shape[::-1], BF16),
            (down_weight.shape, BF16),
        ],
        9,
    )
    pair = [(i, i ^ 1) for i in range(mlp_count)]
    got = lax.ppermute(send, "mlp", pair)
    (chip_half,) = call(add_pair, [((row_count, half), BF16, True)], [], [keep, got])
    others = [
        lax.ppermute(chip_half, "mlp", [(i, (i + shift) % mlp_count) for i in range(mlp_count)])
        for shift in (2, 6, 4)
    ]
    (after_half,) = call(
        add_chips, [((row_count, half), BF16, True)], [], [keep, got, *others, stream_half]
    )
    other_half = lax.ppermute(after_half, "mlp", pair)
    shard_after, next_qkv = call(
        project_next,
        [((row_count, part_width), BF16, False), ((row_count, qkv_weight.shape[1]), BF16, False)],
        [mlp_place.astype(jnp.int32).reshape(1)],
        [after_half, other_half, next_gain.reshape(1, width), qkv_weight],
        scratch=[((row_count, width), F32)],
    )
    return (attended, shard_after, next_qkv)


def solution(mesh):
    return jax.shard_map(
        shards,
        mesh=mesh,
        in_specs=(
            P(("seq", "mlp"), None),
            P(("seq", "mlp"), None),
            P(("seq", "mlp"), None, None),
            P(),
            P(),
            P("seq", "mlp"),
            P(None, "mlp"),
            P(),
            P(None, "mlp"),
            P(None, "mlp"),
            P("mlp", None),
            P(),
            P(None, "mlp"),
        ),
        out_specs=(P(("seq", "mlp"), None), P("seq", "mlp"), P("seq", "mlp")),
        check_vma=False,
    )
```

```python
import functools

import jax
import jax.numpy as jnp
from jax import lax
from jax.experimental import pallas as pl
from jax.experimental.pallas import tpu as pltpu
from jax.sharding import PartitionSpec as P

WINDOW = 2048
NEG_FILL = -1e30
LAST = (((1,), (1,)), ((), ()))
F32 = jnp.float32
BF16 = jnp.bfloat16


def head_major(values, head_dim):
    width = values.shape[1]
    return jnp.concatenate(
        [values[:, start : start + head_dim] for start in range(0, width, head_dim)], axis=0
    )


def put_heads(column, token_count, lanes):
    lane = lax.broadcasted_iota(jnp.int32, (token_count, lanes), 1)
    placed = jnp.zeros((token_count, lanes), F32)
    for head in range(column.shape[0] // token_count):
        part = column[head * token_count : (head + 1) * token_count, :]
        placed = jnp.where(lane == head, part, placed)
    return placed


def send_queries(far_ref, *refs, splits):
    outs, queries_ref, copied = refs[:-2], refs[-2], refs[-1]
    copy = pltpu.make_async_copy(far_ref, queries_ref, copied.at[0])
    copy.start()
    copy.wait()
    for (start, stop), out_ref in zip(splits, outs):
        head_dim = out_ref.shape[2]
        values = queries_ref[:, start * head_dim : stop * head_dim].astype(F32)
        rows = head_major(values, head_dim).astype(BF16)
        for place in range(out_ref.shape[0]):
            out_ref[place] = rows


def attend_new(queries_ref, new_ref, max_ref, sum_ref, acc_ref):
    token_count, width = queries_ref.shape
    head_dim = new_ref.shape[1] // 2
    query = head_major(queries_ref[...].astype(F32), head_dim).astype(BF16)
    scores = lax.dot_general(
        query, new_ref[:, :head_dim], LAST, preferred_element_type=F32
    ) * head_dim ** (-0.5)
    token = lax.broadcasted_iota(jnp.int32, scores.shape, 0) % token_count
    column = lax.broadcasted_iota(jnp.int32, scores.shape, 1)
    valid = column <= token
    peak = jnp.max(jnp.where(valid, scores, NEG_FILL), axis=1, keepdims=True)
    weights = jnp.where(valid, jnp.exp(scores - peak), 0.0)
    rounded = weights.astype(BF16).astype(F32)
    values = new_ref[:, head_dim:].astype(F32)
    acc = jnp.zeros((query.shape[0], head_dim), F32)
    for new in range(token_count):
        acc = acc + rounded[:, new : new + 1] * values[new : new + 1, :]
    max_ref[...] = put_heads(peak, token_count, max_ref.shape[1])
    sum_ref[...] = put_heads(jnp.sum(weights, axis=1, keepdims=True), token_count, sum_ref.shape[1])
    for head in range(width // head_dim):
        acc_ref[:, head * head_dim : (head + 1) * head_dim] = acc[
            head * token_count : (head + 1) * token_count, :
        ]


def attend_pages(
    code_ref, length_ref, rows_ref, front_ref, far_ref, out_ref, score_ref, peak_ref, rest_ref, copied
):
    slot_count, page_len, kv_width = far_ref.shape
    near_count = front_ref.shape[0]
    rest = pltpu.make_async_copy(
        far_ref.at[pl.ds(near_count, slot_count - near_count)], rest_ref, copied.at[0]
    )
    rest.start()

    def cached(slot, span):
        if slot < near_count:
            return front_ref[slot, :, span]
        return rest_ref[slot - near_count, :, span]

    head_dim = kv_width // 2
    token_count = out_ref.shape[1]
    width = out_ref.shape[2] - 128
    query_rows = rows_ref.shape[1]
    head_count = width // head_dim
    page_count = 128
    scale = head_dim ** (-0.5)
    token = lax.broadcasted_iota(jnp.int32, (query_rows, page_len), 0) % token_count
    lane = lax.broadcasted_iota(jnp.int32, (query_rows, page_len), 1)
    low_edge = lane - token + (WINDOW - 1)
    codes = [code_ref[slot] for slot in range(slot_count)]
    sources = [jnp.maximum(code - 1, 0) // page_count for code in codes]
    first = [True] + [
        (codes[slot] == 0) | (codes[slot - 1] == 0) | (sources[slot] != sources[slot - 1])
        for slot in range(1, slot_count)
    ]
    last = first[1:] + [True]
    fill = jnp.full((query_rows, page_len), NEG_FILL, F32)
    peak = fill
    for slot in range(slot_count):
        if slot == near_count:
            rest.wait()
        page = jnp.maximum(codes[slot] - 1, 0) % page_count
        reach = jnp.where(codes[slot] > 0, length_ref[sources[slot]], 0) - page * page_len
        scores = (
            lax.dot_general(
                rows_ref[sources[slot]], cached(slot, slice(0, head_dim)), LAST, preferred_element_type=F32
            )
            * scale
        )
        scores = jnp.where((lane < reach) & (low_edge >= reach), scores, NEG_FILL)
        score_ref[slot] = scores
        peak = jnp.maximum(scores, jnp.where(first[slot], NEG_FILL, peak) if slot else fill)
        peak_ref[slot] = jnp.broadcast_to(jnp.max(peak, axis=1, keepdims=True), (query_rows, page_len))
    for slot in range(slot_count - 2, -1, -1):
        peak_ref[slot] = jnp.where(last[slot], peak_ref[slot], peak_ref[slot + 1])
    total = jnp.zeros((query_rows, page_len), F32)
    acc = jnp.zeros((query_rows, head_dim), F32)
    for slot in range(slot_count):
        weights = jnp.exp(score_ref[slot] - peak_ref[slot])
        value = jnp.dot(weights.astype(BF16), cached(slot, slice(head_dim, kv_width)), preferred_element_type=F32)
        total = weights + (jnp.where(first[slot], 0.0, total) if slot else 0.0)
        acc = value + (jnp.where(first[slot], 0.0, acc) if slot else 0.0)
        finished_total, finished_acc = total, acc

        @pl.when((codes[slot] > 0) & last[slot])
        def _():
            whole_sum = jnp.sum(finished_total, axis=1, keepdims=True)
            result = finished_acc / whole_sum
            for head in range(head_count):
                out_ref[sources[slot], :, head * head_dim : (head + 1) * head_dim] = result[
                    head * token_count : (head + 1) * token_count, :
                ].astype(BF16)
            whole = put_heads(peak_ref[slot][:, :1] + jnp.log(whole_sum), token_count, 128)
            high = whole.astype(BF16).astype(F32)
            middle = (whole - high).astype(BF16).astype(F32)
            low = whole - high - middle
            lanes = lax.broadcasted_iota(jnp.int32, whole.shape, 1)
            packed = jnp.where(
                lanes < 16,
                high,
                jnp.where(lanes < 32, pltpu.roll(middle, 16, 1), pltpu.roll(low, 32, 1)),
            )
            out_ref[sources[slot], :, width:] = packed.astype(BF16)


def merge_new(holder_ref, *refs, splits):
    got_refs = refs[: len(splits)]
    max_ref, sum_ref, acc_ref, attended_ref, spread_ref = refs[len(splits) :]
    holder = holder_ref[0]
    head_dim = 256
    for (first_head, last_head), got_ref in zip(splits, got_refs):
        width = got_ref.shape[2] - 128
        packed = got_ref[holder, :, width:].astype(F32)
        cached = packed + pltpu.roll(packed, 128 - 16, 1) + pltpu.roll(packed, 128 - 32, 1)
        new_max = max_ref[...]
        new_sum = sum_ref[...]
        if first_head:
            new_max = pltpu.roll(new_max, 128 - first_head, 1)
            new_sum = pltpu.roll(new_sum, 128 - first_head, 1)
        peak = jnp.maximum(cached, new_max)
        cached_factor = jnp.exp(cached - peak)
        new_factor = jnp.exp(new_max - peak)
        inverse = 1.0 / (cached_factor + new_factor * new_sum)
        cached_factor = cached_factor * inverse
        new_factor = new_factor * inverse
        for head in range(last_head - first_head):
            whole = slice((first_head + head) * head_dim, (first_head + head + 1) * head_dim)
            rows = (
                got_ref[holder, :, head * head_dim : (head + 1) * head_dim].astype(F32)
                * cached_factor[:, head : head + 1]
                + acc_ref[:, whole] * new_factor[:, head : head + 1]
            ).astype(BF16)
            attended_ref[:, whole] = rows
            for place in range(spread_ref.shape[0]):
                spread_ref[place, :, whole] = rows


def project_out(rows_ref, weight_ref, residual_ref, out_ref):
    places, token_count, width = rows_ref.shape
    rows = jnp.concatenate([rows_ref[place].astype(F32) for place in range(places)], axis=0).astype(BF16)
    attention_out = lax.dot_general(rows, weight_ref[...], LAST, preferred_element_type=F32)
    stream = (residual_ref[...].astype(F32) + attention_out).astype(BF16)
    for place in range(places):
        out_ref[place] = stream


def feed_forward(
    core_ref,
    stream_ref,
    gain_ref,
    gate_ref,
    up_ref,
    down_ref,
    gate_far,
    up_far,
    down_far,
    keep_ref,
    send_ref,
    stream_half_ref,
    whole_ref,
    halves_ref,
    gate_rest,
    up_rest,
    down_rest,
    copied,
):
    parts, rows, width = stream_ref.shape
    total = parts * width
    half = total // 2
    near_rows = gate_ref.shape[0]
    chunks = 2
    step = gate_rest.shape[0] // chunks
    copies = []
    for chunk in range(chunks):
        for far, rest in ((gate_far, gate_rest), (up_far, up_rest), (down_far, down_rest)):
            copies.append(
                pltpu.make_async_copy(
                    far.at[pl.ds(near_rows + chunk * step, step)],
                    rest.at[pl.ds(chunk * step, step)],
                    copied.at[len(copies)],
                )
            )
            copies[-1].start()
    for part in range(parts):
        whole_ref[:, part * width : (part + 1) * width] = stream_ref[part].astype(F32)
    whole = whole_ref[...]
    square = jnp.sum(whole * whole, axis=1, keepdims=True)
    normed = (whole * lax.rsqrt(square / total + 1e-06) * gain_ref[...]).astype(BF16)
    core = core_ref[0]

    @pl.when(core == 0)
    def _():
        stream_half_ref[...] = whole_ref[:, :half]

    @pl.when(core == 1)
    def _():
        stream_half_ref[...] = whole_ref[:, half:]

    def through(gate_rows, up_rows, down_rows):
        gate = lax.dot_general(normed, gate_rows, LAST, preferred_element_type=F32)
        upward = lax.dot_general(normed, up_rows, LAST, preferred_element_type=F32)
        hidden = (jax.nn.gelu(gate, approximate=True) * upward).astype(BF16)
        return jnp.dot(hidden, down_rows, preferred_element_type=F32)

    partial = through(gate_ref[...], up_ref[...], down_ref[...])
    for chunk in range(chunks):
        for copy in copies[3 * chunk : 3 * chunk + 3]:
            copy.wait()
        span = slice(chunk * step, (chunk + 1) * step)
        partial = partial + through(gate_rest[span, :], up_rest[span, :], down_rest[span, :])
    halves_ref[0] = partial[:, :half]
    halves_ref[1] = partial[:, half:]
    keep_ref[...] = halves_ref[core]
    send_ref[...] = halves_ref[1 - core].astype(BF16)


def add_pair(keep_ref, got_ref, send_ref):
    send_ref[...] = (keep_ref[...] + got_ref[...].astype(F32)).astype(BF16)


def add_chips(keep_ref, got_ref, first_ref, second_ref, third_ref, stream_ref, fetched_ref, out_ref):
    total = keep_ref[...] + got_ref[...].astype(F32)
    total = total + first_ref[...].astype(F32) + second_ref[...].astype(F32) + third_ref[...].astype(F32)
    out_ref[...] = (stream_ref[...] + total).astype(BF16)


def project_next(
    place_ref,
    own_ref,
    other_ref,
    gain_ref,
    front_ref,
    weight_far,
    shard_ref,
    out_ref,
    whole_ref,
    rest_ref,
    copied,
):
    rows, half = own_ref.shape
    near_rows = front_ref.shape[0]
    rest = pltpu.make_async_copy(
        weight_far.at[pl.ds(near_rows, rest_ref.shape[0])], rest_ref, copied.at[0]
    )
    rest.start()
    core = place_ref[0] % 2

    @pl.when(core == 0)
    def _():
        whole_ref[:, :half] = own_ref[...].astype(F32)
        whole_ref[:, half:] = other_ref[...].astype(F32)

    @pl.when(core == 1)
    def _():
        whole_ref[:, half:] = own_ref[...].astype(F32)
        whole_ref[:, :half] = other_ref[...].astype(F32)

    part = shard_ref.shape[1]
    for place in range(2 * half // part):

        @pl.when(place_ref[0] == place)
        def _():
            shard_ref[...] = whole_ref[:, place * part : (place + 1) * part].astype(BF16)

    whole = whole_ref[...]
    square = jnp.sum(whole * whole, axis=1, keepdims=True)
    normed = (whole * lax.rsqrt(square / (2 * half) + 1e-06) * gain_ref[...]).astype(BF16)
    front = jnp.dot(normed[:, :near_rows], front_ref[...], preferred_element_type=F32)
    rest.wait()
    back = jnp.dot(normed[:, near_rows:], rest_ref[...], preferred_element_type=F32)
    out_ref[...] = (front + back).astype(BF16)


SMEM = pl.BlockSpec(memory_space=pltpu.SMEM)
VMEM = pl.BlockSpec(memory_space=pltpu.VMEM)
FAR = pl.BlockSpec(memory_space=pl.ANY)


def near(array):
    return pltpu.with_memory_space_constraint(array, pltpu.VMEM)


def call(body, outs, scalars, arrays, far=(), scratch=(), copies=0):
    scratch_shapes = [pltpu.VMEM(shape, dtype) for shape, dtype in scratch]
    if copies:
        scratch_shapes.append(pltpu.SemaphoreType.DMA((copies,)))
    return pl.pallas_call(
        body,
        out_shape=[
            pltpu.VMEM(shape, dtype) if stays else jax.ShapeDtypeStruct(shape, dtype)
            for shape, dtype, stays in outs
        ],
        in_specs=[SMEM] * len(scalars) + [VMEM] * len(arrays) + [FAR] * len(far),
        out_specs=[VMEM] * len(outs),
        scratch_shapes=scratch_shapes,
        name=getattr(body, "func", body).__name__,
    )(*scalars, *[near(array) for array in arrays], *far)


def fetch(parts, after):
    def fetch_rows(*refs):
        fars, outs, copied = refs[1 : 1 + len(parts)], refs[1 + len(parts) : 1 + 2 * len(parts)], refs[-1]
        copies = [
            pltpu.make_async_copy(far.at[pl.ds(0, out.shape[0])], out, copied.at[index])
            for index, (far, out) in enumerate(zip(fars, outs))
        ]
        for copy in copies:
            copy.start()
        for copy in copies:
            copy.wait()

    return pl.pallas_call(
        fetch_rows,
        out_shape=[pltpu.VMEM((rows,) + far.shape[1:], far.dtype) for far, rows in parts]
        + [pltpu.VMEM((8, 128), F32)],
        in_specs=[FAR] * (len(parts) + 1),
        out_specs=[VMEM] * (len(parts) + 1),
        scratch_shapes=[pltpu.SemaphoreType.DMA((len(parts),))],
        name="fetch_rows",
    )(after, *[far for far, _ in parts])


def exchange(copies, axis):
    return lax.all_to_all(copies, axis, split_axis=0, concat_axis=0, tiled=True)


def shards(
    queries,
    new_kv,
    kv_cache,
    lengths,
    page_table,
    residual,
    out_weight,
    norm_gain,
    gate_weight,
    up_weight,
    down_weight,
    next_gain,
    qkv_weight,
):
    seq_count = lax.axis_size("seq")
    mlp_count = lax.axis_size("mlp")
    seq_place = lax.axis_index("seq")
    mlp_place = lax.axis_index("mlp")
    device = seq_place * mlp_count + mlp_place
    slot_count, page_len, kv_width = kv_cache.shape
    head_dim = kv_width // 2
    token_count, width = queries.shape
    page_count = page_table.shape[1]
    row_count, part_width = residual.shape
    half = width // 2

    splits = ((0, width // head_dim),)
    sizes = [token_count * (stop - start) for start, stop in splits]
    sents = call(
        functools.partial(send_queries, splits=splits),
        [((seq_count, size, head_dim), BF16, True) for size in sizes],
        [],
        [],
        [queries],
        [(queries.shape, BF16)],
        1,
    )
    column_rows = [exchange(sent, "seq") for sent in sents]

    column_table = lax.dynamic_index_in_dim(
        page_table.reshape(seq_count, mlp_count, page_count), mlp_place, 1, keepdims=False
    )
    column_lengths = lax.dynamic_index_in_dim(
        lengths.reshape(seq_count, mlp_count), mlp_place, 1, keepdims=False
    )
    entry = (
        jnp.arange(seq_count, dtype=jnp.int32)[:, None] * page_count
        + jnp.arange(page_count, dtype=jnp.int32)[None, :]
        + 1
    )
    slots = device * slot_count + jnp.arange(slot_count, dtype=jnp.int32)
    codes = jnp.max(
        jnp.where(column_table[None] == slots[:, None, None], entry[None], 0), axis=(1, 2)
    )
    own_table = lax.dynamic_index_in_dim(column_table, seq_place, 0, keepdims=False)
    holder = (jnp.max(own_table) // (slot_count * mlp_count)).reshape(1)

    new_max, new_sum, new_acc = call(
        attend_new,
        [((token_count, 128), F32, True)] * 2 + [((token_count, width), F32, True)],
        [],
        [queries, new_kv],
    )
    cache_front, _ = fetch([(kv_cache, 8)], sents[-1])
    returned = []
    for arrived in column_rows:
        (held,) = call(
            attend_pages,
            [((seq_count, token_count, arrived.shape[1] // token_count * head_dim + 128), BF16, True)],
            [codes, column_lengths],
            [arrived, cache_front],
            [kv_cache],
            [((slot_count, arrived.shape[1], page_len), F32)] * 2
            + [((slot_count - 8, page_len, kv_width), BF16)],
            1,
        )
        returned.append(exchange(held, "seq"))
    attended, spread = call(
        functools.partial(merge_new, splits=splits),
        [((token_count, width), BF16, False), ((mlp_count, token_count, width), BF16, True)],
        [holder],
        [*returned, new_max, new_sum, new_acc],
    )
    rows = exchange(spread, "mlp")
    (streams,) = call(
        project_out,
        [((mlp_count, row_count, part_width), BF16, True)],
        [],
        [rows, *fetch([(out_weight.T, part_width)], held)[:-1], residual],
    )
    layers = [(gate_weight.T, 128), (up_weight.T, 128), (down_weight, 128)]
    *front, _ = fetch(layers, streams)
    streams = exchange(streams, "mlp")

    core = (mlp_place % 2).astype(jnp.int32).reshape(1)
    keep, send, stream_half = call(
        feed_forward,
        [((row_count, half), F32, True), ((row_count, half), BF16, True), ((row_count, half), F32, True)],
        [core],
        [streams, norm_gain.reshape(1, width), *front],
        [far for far, _ in layers],
        [((row_count, width), F32), ((2, row_count, half), F32)]
        + [((far.shape[0] - rows, width), BF16) for far, rows in layers],
        6,
    )
    pair = [(i, i ^ 1) for i in range(mlp_count)]
    got = lax.ppermute(send, "mlp", pair)
    (chip_half,) = call(add_pair, [((row_count, half), BF16, True)], [], [keep, got])
    others = [
        lax.ppermute(chip_half, "mlp", [(i, (i + shift) % mlp_count) for i in range(mlp_count)])
        for shift in (2, 6, 4)
    ]
    near_rows = 1664
    qkv_front, fetched = fetch([(qkv_weight, near_rows)], chip_half)
    (after_half,) = call(
        add_chips, [((row_count, half), BF16, True)], [], [keep, got, *others, stream_half], [fetched]
    )
    other_half = lax.ppermute(after_half, "mlp", pair)
    shard_after, next_qkv = call(
        project_next,
        [((row_count, part_width), BF16, False), ((row_count, qkv_weight.shape[1]), BF16, False)],
        [mlp_place.astype(jnp.int32).reshape(1)],
        [after_half, other_half, next_gain.reshape(1, width), qkv_front],
        [qkv_weight],
        [((row_count, width), F32), ((width - near_rows, qkv_weight.shape[1]), BF16)],
        1,
    )
    return (attended, shard_after, next_qkv)


def solution(mesh):
    return jax.shard_map(
        shards,
        mesh=mesh,
        in_specs=(
            P(("seq", "mlp"), None),
            P(("seq", "mlp"), None),
            P(("seq", "mlp"), None, None),
            P(),
            P(),
            P("seq", "mlp"),
            P(None, "mlp"),
            P(),
            P(None, "mlp"),
            P(None, "mlp"),
            P("mlp", None),
            P(),
            P(None, "mlp"),
        ),
        out_specs=(P(("seq", "mlp"), None), P("seq", "mlp"), P("seq", "mlp")),
        check_vma=False,
    )
```

```python
import functools

import jax
import jax.numpy as jnp
from jax import lax
from jax.experimental import pallas as pl
from jax.experimental.pallas import tpu as pltpu
from jax.sharding import PartitionSpec as P

WINDOW = 2048
NEG_FILL = -1e30
LAST = (((1,), (1,)), ((), ()))
F32 = jnp.float32
BF16 = jnp.bfloat16


def head_major(values, head_dim):
    width = values.shape[1]
    return jnp.concatenate(
        [values[:, start : start + head_dim] for start in range(0, width, head_dim)], axis=0
    )


def put_heads(column, token_count, lanes):
    lane = lax.broadcasted_iota(jnp.int32, (token_count, lanes), 1)
    placed = jnp.zeros((token_count, lanes), F32)
    for head in range(column.shape[0] // token_count):
        part = column[head * token_count : (head + 1) * token_count, :]
        placed = jnp.where(lane == head, part, placed)
    return placed


def send_queries(queries_ref, out_ref):
    rows = head_major(queries_ref[...].astype(F32), out_ref.shape[2]).astype(BF16)
    for place in range(out_ref.shape[0]):
        out_ref[place] = rows


def attend_new(queries_ref, new_ref, max_ref, sum_ref, acc_ref):
    token_count, width = queries_ref.shape
    head_dim = new_ref.shape[1] // 2
    query = head_major(queries_ref[...].astype(F32), head_dim).astype(BF16)
    scores = lax.dot_general(
        query, new_ref[:, :head_dim], LAST, preferred_element_type=F32
    ) * head_dim ** (-0.5)
    token = lax.broadcasted_iota(jnp.int32, scores.shape, 0) % token_count
    column = lax.broadcasted_iota(jnp.int32, scores.shape, 1)
    valid = column <= token
    peak = jnp.max(jnp.where(valid, scores, NEG_FILL), axis=1, keepdims=True)
    weights = jnp.where(valid, jnp.exp(scores - peak), 0.0)
    rounded = weights.astype(BF16).astype(F32)
    values = new_ref[:, head_dim:].astype(F32)
    acc = jnp.zeros((query.shape[0], head_dim), F32)
    for new in range(token_count):
        acc = acc + rounded[:, new : new + 1] * values[new : new + 1, :]
    max_ref[...] = put_heads(peak, token_count, max_ref.shape[1])
    sum_ref[...] = put_heads(jnp.sum(weights, axis=1, keepdims=True), token_count, sum_ref.shape[1])
    for head in range(width // head_dim):
        acc_ref[:, head * head_dim : (head + 1) * head_dim] = acc[
            head * token_count : (head + 1) * token_count, :
        ]


def attend_pages(
    code_ref, length_ref, rows_ref, front_ref, far_ref, out_ref, score_ref, peak_ref, acc_ref, rest_ref, end_ref, copied
):
    slot_count, page_len, kv_width = far_ref.shape
    near_count = front_ref.shape[0]
    rest = pltpu.make_async_copy(
        far_ref.at[pl.ds(near_count, slot_count - near_count)], rest_ref, copied.at[0]
    )
    rest.start()

    def cached(slot, span):
        if slot < near_count:
            return front_ref[slot, :, span]
        return rest_ref[slot - near_count, :, span]

    head_dim = kv_width // 2
    token_count = out_ref.shape[1]
    width = out_ref.shape[2] - 128
    query_rows = rows_ref.shape[1]
    head_count = width // head_dim
    page_count = 128
    scale = head_dim ** (-0.5)
    token = lax.broadcasted_iota(jnp.int32, (query_rows, page_len), 0) % token_count
    lane = lax.broadcasted_iota(jnp.int32, (query_rows, page_len), 1)
    low_edge = lane - token + (WINDOW - 1)
    codes = [code_ref[slot] for slot in range(slot_count)]
    sources = [jnp.maximum(code - 1, 0) // page_count for code in codes]
    first = [True] + [
        (codes[slot] == 0) | (codes[slot - 1] == 0) | (sources[slot] != sources[slot - 1])
        for slot in range(1, slot_count)
    ]
    last = first[1:] + [True]
    fill = jnp.full((query_rows, page_len), NEG_FILL, F32)
    peak = fill
    for slot in range(slot_count):
        if slot == near_count:
            rest.wait()
        page = jnp.maximum(codes[slot] - 1, 0) % page_count
        reach = jnp.where(codes[slot] > 0, length_ref[sources[slot]], 0) - page * page_len
        scores = (
            lax.dot_general(
                rows_ref[sources[slot]], cached(slot, slice(0, head_dim)), LAST, preferred_element_type=F32
            )
            * scale
        )
        scores = jnp.where((lane < reach) & (low_edge >= reach), scores, NEG_FILL)
        score_ref[slot] = scores
        peak = jnp.maximum(scores, jnp.where(first[slot], NEG_FILL, peak) if slot else fill)
        peak_ref[slot] = jnp.broadcast_to(jnp.max(peak, axis=1, keepdims=True), (query_rows, page_len))
    peak = peak_ref[slot_count - 1]
    for slot in range(slot_count - 2, -1, -1):
        peak = jnp.where(last[slot], peak_ref[slot], peak)
        peak_ref[slot] = peak
    total = jnp.zeros((query_rows, page_len), F32)
    acc = jnp.zeros((query_rows, head_dim), F32)
    held = jnp.int32(0)
    for slot in range(slot_count):
        weights = jnp.exp(score_ref[slot] - peak_ref[slot])
        value = jnp.dot(
            weights.astype(BF16), cached(slot, slice(head_dim, kv_width)), preferred_element_type=F32
        )
        total = weights + (jnp.where(first[slot], 0.0, total) if slot else 0.0)
        acc = value + (jnp.where(first[slot], 0.0, acc) if slot else 0.0)
        score_ref[slot] = total
        acc_ref[slot] = acc
        end_ref[held] = slot
        held = held + ((codes[slot] > 0) & last[slot]).astype(jnp.int32)
    lanes = lax.broadcasted_iota(jnp.int32, (token_count, 128), 1)
    for turn in range(slot_count // 2):
        slot = end_ref[jnp.where(turn < held, turn, 0)]
        source = jnp.maximum(code_ref[slot] - 1, 0) // page_count
        whole_sum = jnp.sum(score_ref[slot], axis=1, keepdims=True)
        result = acc_ref[slot] / whole_sum
        for head in range(head_count):
            out_ref[source, :, head * head_dim : (head + 1) * head_dim] = result[
                head * token_count : (head + 1) * token_count, :
            ].astype(BF16)
        whole = put_heads(peak_ref[slot][:, :1] + jnp.log(whole_sum), token_count, 128)
        high = whole.astype(BF16).astype(F32)
        middle = (whole - high).astype(BF16).astype(F32)
        low = whole - high - middle
        packed = jnp.where(
            lanes < 16, high, jnp.where(lanes < 32, pltpu.roll(middle, 16, 1), pltpu.roll(low, 32, 1))
        )
        out_ref[source, :, width:] = packed.astype(BF16)


def merge_new(holder_ref, *refs, splits):
    got_refs = refs[: len(splits)]
    max_ref, sum_ref, acc_ref, attended_ref, spread_ref = refs[len(splits) :]
    holder = holder_ref[0]
    head_dim = 256
    for (first_head, last_head), got_ref in zip(splits, got_refs):
        width = got_ref.shape[2] - 128
        packed = got_ref[holder, :, width:].astype(F32)
        cached = packed + pltpu.roll(packed, 128 - 16, 1) + pltpu.roll(packed, 128 - 32, 1)
        new_max = max_ref[...]
        new_sum = sum_ref[...]
        if first_head:
            new_max = pltpu.roll(new_max, 128 - first_head, 1)
            new_sum = pltpu.roll(new_sum, 128 - first_head, 1)
        peak = jnp.maximum(cached, new_max)
        cached_factor = jnp.exp(cached - peak)
        new_factor = jnp.exp(new_max - peak)
        inverse = 1.0 / (cached_factor + new_factor * new_sum)
        cached_factor = cached_factor * inverse
        new_factor = new_factor * inverse
        for head in range(last_head - first_head):
            whole = slice((first_head + head) * head_dim, (first_head + head + 1) * head_dim)
            rows = (
                got_ref[holder, :, head * head_dim : (head + 1) * head_dim].astype(F32)
                * cached_factor[:, head : head + 1]
                + acc_ref[:, whole] * new_factor[:, head : head + 1]
            ).astype(BF16)
            attended_ref[:, whole] = rows
            for place in range(spread_ref.shape[0]):
                spread_ref[place, :, whole] = rows


def project_out(rows_ref, residual_ref, front_ref, weight_far, out_ref, rest_ref, copied):
    places = rows_ref.shape[0]
    near_rows = front_ref.shape[0]
    rest = pltpu.make_async_copy(weight_far.at[pl.ds(near_rows, rest_ref.shape[0])], rest_ref, copied.at[0])
    rest.start()
    rows = jnp.concatenate([rows_ref[place].astype(F32) for place in range(places)], axis=0).astype(BF16)
    attention_out = lax.dot_general(rows, front_ref[...], LAST, preferred_element_type=F32)
    out_ref[:, :near_rows] = (residual_ref[:, :near_rows].astype(F32) + attention_out).astype(BF16)
    rest.wait()
    attention_out = lax.dot_general(rows, rest_ref[...], LAST, preferred_element_type=F32)
    out_ref[:, near_rows:] = (residual_ref[:, near_rows:].astype(F32) + attention_out).astype(BF16)


def feed_forward(place_ref, *refs):
    block_refs = refs[:8]
    gain_ref, gate_ref, up_ref, down_ref, gate_far, up_far, down_far = refs[8:15]
    keep_ref, send_ref, base_ref = refs[15:18]
    stream_ref, whole_ref, halves_ref, gate_rest, up_rest, down_rest, copied = refs[18:]
    parts, rows, width = stream_ref.shape
    total = parts * width
    half = total // 2
    near_rows = gate_ref.shape[0]
    chunks = 2
    step = gate_rest.shape[0] // chunks
    copies = []
    for chunk in range(chunks):
        for far, rest in ((gate_far, gate_rest), (up_far, up_rest), (down_far, down_rest)):
            copies.append(
                pltpu.make_async_copy(
                    far.at[pl.ds(near_rows + chunk * step, step)],
                    rest.at[pl.ds(chunk * step, step)],
                    copied.at[len(copies)],
                )
            )
            copies[-1].start()
    for distance, block_ref in enumerate(block_refs):
        stream_ref[place_ref[0] ^ distance] = block_ref[...].astype(F32)
    for part in range(parts):
        whole_ref[:, part * width : (part + 1) * width] = stream_ref[part]
    whole = whole_ref[...]
    square = jnp.sum(whole * whole, axis=1, keepdims=True)
    normed = (whole * lax.rsqrt(square / total + 1e-06) * gain_ref[...]).astype(BF16)
    core = place_ref[0] % 2

    def through(gate_rows, up_rows, down_rows):
        gate = lax.dot_general(normed, gate_rows, LAST, preferred_element_type=F32)
        upward = lax.dot_general(normed, up_rows, LAST, preferred_element_type=F32)
        hidden = (jax.nn.gelu(gate, approximate=True) * upward).astype(BF16)
        return jnp.dot(hidden, down_rows, preferred_element_type=F32)

    partial = through(gate_ref[...], up_ref[...], down_ref[...])
    for chunk in range(chunks):
        for copy in copies[3 * chunk : 3 * chunk + 3]:
            copy.wait()
        span = slice(chunk * step, (chunk + 1) * step)
        partial = partial + through(gate_rest[span, :], up_rest[span, :], down_rest[span, :])
    halves_ref[0] = partial[:, :half]
    halves_ref[1] = partial[:, half:]
    keep_ref[...] = halves_ref[core]
    send_ref[...] = halves_ref[1 - core].astype(BF16)

    @pl.when(core == 0)
    def _():
        base_ref[...] = whole_ref[:, :half] + keep_ref[...]

    @pl.when(core == 1)
    def _():
        base_ref[...] = whole_ref[:, half:] + keep_ref[...]


def add_pair(keep_ref, got_ref, send_ref):
    send_ref[...] = (keep_ref[...] + got_ref[...].astype(F32)).astype(BF16)


def add_chips(base_ref, got_ref, first_ref, second_ref, third_ref, fetched_ref, out_ref):
    total = base_ref[...] + got_ref[...].astype(F32)
    total = total + first_ref[...].astype(F32) + second_ref[...].astype(F32) + third_ref[...].astype(F32)
    out_ref[...] = total.astype(BF16)


def project_next(
    place_ref,
    own_ref,
    other_ref,
    gain_ref,
    front_ref,
    weight_far,
    shard_ref,
    out_ref,
    whole_ref,
    rest_ref,
    copied,
):
    rows, half = own_ref.shape
    near_rows = front_ref.shape[0]
    rest = pltpu.make_async_copy(
        weight_far.at[pl.ds(near_rows, rest_ref.shape[0])], rest_ref, copied.at[0]
    )
    rest.start()
    core = place_ref[0] % 2

    @pl.when(core == 0)
    def _():
        whole_ref[:, :half] = own_ref[...].astype(F32)
        whole_ref[:, half:] = other_ref[...].astype(F32)

    @pl.when(core == 1)
    def _():
        whole_ref[:, half:] = own_ref[...].astype(F32)
        whole_ref[:, :half] = other_ref[...].astype(F32)

    part = shard_ref.shape[1]
    for place in range(2 * half // part):

        @pl.when(place_ref[0] == place)
        def _():
            shard_ref[...] = whole_ref[:, place * part : (place + 1) * part].astype(BF16)

    whole = whole_ref[...]
    square = jnp.sum(whole * whole, axis=1, keepdims=True)
    normed = (whole * lax.rsqrt(square / (2 * half) + 1e-06) * gain_ref[...]).astype(BF16)
    front = jnp.dot(normed[:, :near_rows], front_ref[...], preferred_element_type=F32)
    rest.wait()
    back = jnp.dot(normed[:, near_rows:], rest_ref[...], preferred_element_type=F32)
    out_ref[...] = (front + back).astype(BF16)


SMEM = pl.BlockSpec(memory_space=pltpu.SMEM)
VMEM = pl.BlockSpec(memory_space=pltpu.VMEM)
FAR = pl.BlockSpec(memory_space=pl.ANY)


def near(array):
    return pltpu.with_memory_space_constraint(array, pltpu.VMEM)


def call(body, outs, scalars, arrays, far=(), scratch=(), copies=0, more=()):
    scratch_shapes = [pltpu.VMEM(shape, dtype) for shape, dtype in scratch] + list(more)
    if copies:
        scratch_shapes.append(pltpu.SemaphoreType.DMA((copies,)))
    return pl.pallas_call(
        body,
        out_shape=[
            pltpu.VMEM(shape, dtype) if stays else jax.ShapeDtypeStruct(shape, dtype)
            for shape, dtype, stays in outs
        ],
        in_specs=[SMEM] * len(scalars) + [VMEM] * len(arrays) + [FAR] * len(far),
        out_specs=[VMEM] * len(outs),
        scratch_shapes=scratch_shapes,
        name=getattr(body, "func", body).__name__,
    )(*scalars, *[near(array) for array in arrays], *far)


def fetch(parts, after):
    def fetch_rows(*refs):
        fars, outs, copied = refs[1 : 1 + len(parts)], refs[1 + len(parts) : 1 + 2 * len(parts)], refs[-1]
        copies = [
            pltpu.make_async_copy(far.at[pl.ds(0, out.shape[0])], out, copied.at[index])
            for index, (far, out) in enumerate(zip(fars, outs))
        ]
        for copy in copies:
            copy.start()
        for copy in copies:
            copy.wait()

    return pl.pallas_call(
        fetch_rows,
        out_shape=[pltpu.VMEM((rows,) + far.shape[1:], far.dtype) for far, rows in parts]
        + [jax.ShapeDtypeStruct((8, 128), F32)],
        in_specs=[FAR] * (len(parts) + 1),
        out_specs=[VMEM] * (len(parts) + 1),
        scratch_shapes=[pltpu.SemaphoreType.DMA((len(parts),))],
        name="fetch_rows",
    )(after, *[far for far, _ in parts])


def exchange(copies, axis):
    return lax.all_to_all(copies, axis, split_axis=0, concat_axis=0, tiled=True)


def partner(block, distance):
    count = lax.axis_size("mlp")
    return lax.ppermute(block, "mlp", [(i, i ^ distance) for i in range(count)])


def gather(block):
    near = {0: block, **{distance: partner(block, distance) for distance in (2, 6, 4)}}
    far = {distance ^ 1: partner(near[distance], 1) for distance in near}
    return [{**near, **far}[distance] for distance in range(8)]


def shards(
    queries,
    new_kv,
    kv_cache,
    lengths,
    page_table,
    residual,
    out_weight,
    norm_gain,
    gate_weight,
    up_weight,
    down_weight,
    next_gain,
    qkv_weight,
):
    seq_count = lax.axis_size("seq")
    mlp_count = lax.axis_size("mlp")
    seq_place = lax.axis_index("seq")
    mlp_place = lax.axis_index("mlp")
    device = seq_place * mlp_count + mlp_place
    slot_count, page_len, kv_width = kv_cache.shape
    head_dim = kv_width // 2
    token_count, width = queries.shape
    page_count = page_table.shape[1]
    row_count, part_width = residual.shape
    half = width // 2

    splits = ((0, width // head_dim),)
    query_rows = token_count * (width // head_dim)
    sent = pl.pallas_call(
        send_queries,
        out_shape=jax.ShapeDtypeStruct((seq_count, query_rows, head_dim), BF16),
        in_specs=[VMEM],
        out_specs=VMEM,
        name="send_queries",
    )(queries)
    sents = [sent]
    column_rows = [exchange(sent, "seq")]

    column_table = lax.dynamic_index_in_dim(
        page_table.reshape(seq_count, mlp_count, page_count), mlp_place, 1, keepdims=False
    )
    column_lengths = lax.dynamic_index_in_dim(
        lengths.reshape(seq_count, mlp_count), mlp_place, 1, keepdims=False
    )
    entry = (
        jnp.arange(seq_count, dtype=jnp.int32)[:, None] * page_count
        + jnp.arange(page_count, dtype=jnp.int32)[None, :]
        + 1
    )
    slots = device * slot_count + jnp.arange(slot_count, dtype=jnp.int32)
    codes = jnp.max(
        jnp.where(column_table[None] == slots[:, None, None], entry[None], 0), axis=(1, 2)
    )
    own_table = lax.dynamic_index_in_dim(column_table, seq_place, 0, keepdims=False)
    holder = (jnp.max(own_table) // (slot_count * mlp_count)).reshape(1)

    new_max, new_sum, new_acc = call(
        attend_new,
        [((token_count, 128), F32, True)] * 2 + [((token_count, width), F32, True)],
        [],
        [queries, new_kv],
    )
    near_slots = 11
    cache_front, _ = fetch([(kv_cache, near_slots)], sents[-1])
    returned = []
    for arrived in column_rows:
        (held,) = call(
            attend_pages,
            [((seq_count, token_count, arrived.shape[1] // token_count * head_dim + 128), BF16, False)],
            [codes, column_lengths],
            [arrived, cache_front],
            [kv_cache],
            [((slot_count, arrived.shape[1], page_len), F32)] * 2
            + [((slot_count, arrived.shape[1], head_dim), F32)]
            + [((slot_count - near_slots, page_len, kv_width), BF16)],
            1,
            [pltpu.SMEM((slot_count + 1,), jnp.int32)],
        )
        returned.append(exchange(held, "seq"))
    attended, spread = call(
        functools.partial(merge_new, splits=splits),
        [((token_count, width), BF16, False), ((mlp_count, token_count, width), BF16, True)],
        [holder],
        [*returned, new_max, new_sum, new_acc],
    )
    rows = exchange(spread, "mlp")
    layers = [(gate_weight.T, 96), (up_weight.T, 96), (down_weight, 96)]
    out_front, *front, _ = fetch([(out_weight.T, 128), *layers], held)
    (stream,) = call(
        project_out,
        [((row_count, part_width), BF16, True)],
        [],
        [rows, residual, out_front],
        [out_weight.T],
        [((part_width - 128, width), BF16)],
        1,
    )
    place = mlp_place.astype(jnp.int32).reshape(1)
    keep, send, base = call(
        feed_forward,
        [((row_count, half), F32, True), ((row_count, half), BF16, True), ((row_count, half), F32, True)],
        [place],
        [*gather(stream), norm_gain.reshape(1, width), *front],
        [far for far, _ in layers],
        [
            ((mlp_count, row_count, part_width), F32),
            ((row_count, width), F32),
            ((2, row_count, half), F32),
        ]
        + [((far.shape[0] - rows, width), BF16) for far, rows in layers],
        6,
    )
    got = partner(send, 1)
    (chip_half,) = call(add_pair, [((row_count, half), BF16, True)], [], [keep, got])
    others = [partner(chip_half, distance) for distance in (2, 6, 4)]
    near_rows = 1536
    qkv_front, fetched = fetch([(qkv_weight, near_rows)], held)
    (after_half,) = call(
        add_chips, [((row_count, half), BF16, True)], [], [base, got, *others], [fetched]
    )
    other_half = partner(after_half, 1)
    shard_after, next_qkv = call(
        project_next,
        [((row_count, part_width), BF16, False), ((row_count, qkv_weight.shape[1]), BF16, False)],
        [place],
        [after_half, other_half, next_gain.reshape(1, width), qkv_front],
        [qkv_weight],
        [((row_count, width), F32), ((width - near_rows, qkv_weight.shape[1]), BF16)],
        1,
    )
    return (attended, shard_after, next_qkv)


def solution(mesh):
    return jax.shard_map(
        shards,
        mesh=mesh,
        in_specs=(
            P(("seq", "mlp"), None),
            P(("seq", "mlp"), None),
            P(("seq", "mlp"), None, None),
            P(),
            P(),
            P("seq", "mlp"),
            P(None, "mlp"),
            P(),
            P(None, "mlp"),
            P(None, "mlp"),
            P("mlp", None),
            P(),
            P(None, "mlp"),
        ),
        out_specs=(P(("seq", "mlp"), None), P("seq", "mlp"), P("seq", "mlp")),
        check_vma=False,
    )
```

```python
import jax
import jax.numpy as jnp
from jax import lax
from jax.experimental import pallas as pl
from jax.experimental.pallas import tpu as pltpu
from jax.sharding import PartitionSpec as P

WINDOW = 2048
NEG_FILL = -1e30
LAST = (((1,), (1,)), ((), ()))
F32 = jnp.float32
BF16 = jnp.bfloat16


def head_major(values, head_dim):
    width = values.shape[1]
    return jnp.concatenate(
        [values[:, start : start + head_dim] for start in range(0, width, head_dim)], axis=0
    )


def put_heads(column, token_count, lanes):
    lane = lax.broadcasted_iota(jnp.int32, (token_count, lanes), 1)
    placed = jnp.zeros((token_count, lanes), F32)
    for head in range(column.shape[0] // token_count):
        part = column[head * token_count : (head + 1) * token_count, :]
        placed = jnp.where(lane == head, part, placed)
    return placed


def copy_queries(queries_ref, out_ref):
    queries = queries_ref[...]
    for place in range(out_ref.shape[0]):
        out_ref[place] = queries


def attend_new(queries_ref, new_ref, max_ref, sum_ref, acc_ref):
    token_count, width = queries_ref.shape
    head_dim = new_ref.shape[1] // 2
    query = head_major(queries_ref[...].astype(F32), head_dim).astype(BF16)
    scores = lax.dot_general(
        query, new_ref[:, :head_dim], LAST, preferred_element_type=F32
    ) * head_dim ** (-0.5)
    token = lax.broadcasted_iota(jnp.int32, scores.shape, 0) % token_count
    column = lax.broadcasted_iota(jnp.int32, scores.shape, 1)
    valid = column <= token
    peak = jnp.max(jnp.where(valid, scores, NEG_FILL), axis=1, keepdims=True)
    weights = jnp.where(valid, jnp.exp(scores - peak), 0.0)
    rounded = weights.astype(BF16).astype(F32)
    values = new_ref[:, head_dim:].astype(F32)
    acc = jnp.zeros((query.shape[0], head_dim), F32)
    for new in range(token_count):
        acc = acc + rounded[:, new : new + 1] * values[new : new + 1, :]
    max_ref[...] = put_heads(peak, token_count, max_ref.shape[1])
    sum_ref[...] = put_heads(jnp.sum(weights, axis=1, keepdims=True), token_count, sum_ref.shape[1])
    for head in range(width // head_dim):
        acc_ref[:, head * head_dim : (head + 1) * head_dim] = acc[
            head * token_count : (head + 1) * token_count, :
        ]


def attend_pages(
    code_ref, length_ref, rows_ref, front_ref, far_ref, out_ref, score_ref, peak_ref, acc_ref, rest_ref, end_ref, copied
):
    slot_count, page_len, kv_width = far_ref.shape
    near_count = front_ref.shape[0]
    rest = pltpu.make_async_copy(
        far_ref.at[pl.ds(near_count, slot_count - near_count)], rest_ref, copied.at[0]
    )
    rest.start()

    def cached(slot, span):
        if slot < near_count:
            return front_ref[slot, :, span]
        return rest_ref[slot - near_count, :, span]

    head_dim = kv_width // 2
    token_count = out_ref.shape[1]
    width = out_ref.shape[2] - 128
    query_rows = token_count * (width // head_dim)
    head_count = width // head_dim
    page_count = 128
    scale = head_dim ** (-0.5)
    token = lax.broadcasted_iota(jnp.int32, (query_rows, page_len), 0) % token_count
    lane = lax.broadcasted_iota(jnp.int32, (query_rows, page_len), 1)
    low_edge = lane - token + (WINDOW - 1)
    codes = [code_ref[slot] for slot in range(slot_count)]
    sources = [jnp.maximum(code - 1, 0) // page_count for code in codes]
    first = [True] + [
        (codes[slot] == 0) | (codes[slot - 1] == 0) | (sources[slot] != sources[slot - 1])
        for slot in range(1, slot_count)
    ]
    last = first[1:] + [True]
    fill = jnp.full((query_rows, page_len), NEG_FILL, F32)
    peak = fill
    for slot in range(slot_count):
        if slot == near_count:
            rest.wait()
        page = jnp.maximum(codes[slot] - 1, 0) % page_count
        reach = jnp.where(codes[slot] > 0, length_ref[sources[slot]], 0) - page * page_len
        scores = (
            lax.dot_general(
                head_major(rows_ref[sources[slot]].astype(F32), head_dim).astype(BF16),
                cached(slot, slice(0, head_dim)),
                LAST, preferred_element_type=F32
            )
            * scale
        )
        scores = jnp.where((lane < reach) & (low_edge >= reach), scores, NEG_FILL)
        score_ref[slot] = scores
        peak = jnp.maximum(scores, jnp.where(first[slot], NEG_FILL, peak) if slot else fill)
        peak_ref[slot] = jnp.broadcast_to(jnp.max(peak, axis=1, keepdims=True), (query_rows, page_len))
    peak = peak_ref[slot_count - 1]
    for slot in range(slot_count - 2, -1, -1):
        peak = jnp.where(last[slot], peak_ref[slot], peak)
        peak_ref[slot] = peak
    total = jnp.zeros((query_rows, page_len), F32)
    acc = jnp.zeros((query_rows, head_dim), F32)
    held = jnp.int32(0)
    for slot in range(slot_count):
        weights = jnp.exp(score_ref[slot] - peak_ref[slot])
        value = jnp.dot(
            weights.astype(BF16), cached(slot, slice(head_dim, kv_width)), preferred_element_type=F32
        )
        total = weights + (jnp.where(first[slot], 0.0, total) if slot else 0.0)
        acc = value + (jnp.where(first[slot], 0.0, acc) if slot else 0.0)
        score_ref[slot] = total
        acc_ref[slot] = acc
        end_ref[held] = slot
        held = held + ((codes[slot] > 0) & last[slot]).astype(jnp.int32)
    lanes = lax.broadcasted_iota(jnp.int32, (token_count, 128), 1)
    for turn in range(slot_count // 2):
        slot = end_ref[jnp.where(turn < held, turn, 0)]
        source = jnp.maximum(code_ref[slot] - 1, 0) // page_count
        whole_sum = jnp.sum(score_ref[slot], axis=1, keepdims=True)
        result = acc_ref[slot] / whole_sum
        for head in range(head_count):
            out_ref[source, :, head * head_dim : (head + 1) * head_dim] = result[
                head * token_count : (head + 1) * token_count, :
            ].astype(BF16)
        whole = put_heads(peak_ref[slot][:, :1] + jnp.log(whole_sum), token_count, 128)
        high = whole.astype(BF16).astype(F32)
        middle = (whole - high).astype(BF16).astype(F32)
        low = whole - high - middle
        packed = jnp.where(
            lanes < 16, high, jnp.where(lanes < 32, pltpu.roll(middle, 16, 1), pltpu.roll(low, 32, 1))
        )
        out_ref[source, :, width:] = packed.astype(BF16)


def merge_new(holder_ref, got_ref, max_ref, sum_ref, acc_ref, attended_ref, spread_ref):
    holder = holder_ref[0]
    head_dim = 256
    width = attended_ref.shape[1]
    packed = got_ref[holder, :, width:].astype(F32)
    cached = packed + pltpu.roll(packed, 128 - 16, 1) + pltpu.roll(packed, 128 - 32, 1)
    new_max = max_ref[...]
    peak = jnp.maximum(cached, new_max)
    cached_factor = jnp.exp(cached - peak)
    new_factor = jnp.exp(new_max - peak)
    inverse = 1.0 / (cached_factor + new_factor * sum_ref[...])
    cached_factor = cached_factor * inverse
    new_factor = new_factor * inverse
    for head in range(width // head_dim):
        span = slice(head * head_dim, (head + 1) * head_dim)
        rows = (
            got_ref[holder, :, span].astype(F32) * cached_factor[:, head : head + 1]
            + acc_ref[:, span] * new_factor[:, head : head + 1]
        ).astype(BF16)
        attended_ref[:, span] = rows
        for place in range(spread_ref.shape[0]):
            spread_ref[place, :, span] = rows


def project_out(rows_ref, residual_ref, front_ref, weight_far, out_ref, rest_ref, copied):
    places = rows_ref.shape[0]
    near_rows = front_ref.shape[0]
    rest = pltpu.make_async_copy(weight_far.at[pl.ds(near_rows, rest_ref.shape[0])], rest_ref, copied.at[0])
    rest.start()
    rows = jnp.concatenate([rows_ref[place].astype(F32) for place in range(places)], axis=0).astype(BF16)
    attention_out = lax.dot_general(rows, front_ref[...], LAST, preferred_element_type=F32)
    out_ref[:, :near_rows] = (residual_ref[:, :near_rows].astype(F32) + attention_out).astype(BF16)
    rest.wait()
    attention_out = lax.dot_general(rows, rest_ref[...], LAST, preferred_element_type=F32)
    out_ref[:, near_rows:] = (residual_ref[:, near_rows:].astype(F32) + attention_out).astype(BF16)


def feed_forward(place_ref, *refs):
    block_refs = refs[:8]
    gain_ref, gate_ref, up_ref, down_ref, gate_far, up_far, down_far = refs[8:15]
    keep_ref, send_ref, base_ref = refs[15:18]
    stream_ref, whole_ref, halves_ref, gate_rest, up_rest, down_rest, copied = refs[18:]
    parts, rows, width = stream_ref.shape
    total = parts * width
    half = total // 2
    near_rows = gate_ref.shape[0]
    chunks = copied.shape[0] // 3
    step = gate_rest.shape[0] // chunks
    copies = []
    for chunk in range(chunks):
        for far, rest in ((gate_far, gate_rest), (up_far, up_rest), (down_far, down_rest)):
            copies.append(
                pltpu.make_async_copy(
                    far.at[pl.ds(near_rows + chunk * step, step)],
                    rest.at[pl.ds(chunk * step, step)],
                    copied.at[len(copies)],
                )
            )
            copies[-1].start()
    for distance, block_ref in enumerate(block_refs):
        stream_ref[place_ref[0] ^ distance] = block_ref[...].astype(F32)
    for part in range(parts):
        whole_ref[:, part * width : (part + 1) * width] = stream_ref[part]
    whole = whole_ref[...]
    square = jnp.sum(whole * whole, axis=1, keepdims=True)
    normed = (whole * lax.rsqrt(square / total + 1e-06) * gain_ref[...]).astype(BF16)
    core = place_ref[0] % 2

    def through(gate_rows, up_rows, down_rows):
        gate = lax.dot_general(normed, gate_rows, LAST, preferred_element_type=F32)
        upward = lax.dot_general(normed, up_rows, LAST, preferred_element_type=F32)
        hidden = (jax.nn.gelu(gate, approximate=True) * upward).astype(BF16)
        return jnp.dot(hidden, down_rows, preferred_element_type=F32)

    partial = through(gate_ref[...], up_ref[...], down_ref[...])
    for chunk in range(chunks):
        for copy in copies[3 * chunk : 3 * chunk + 3]:
            copy.wait()
        span = slice(chunk * step, (chunk + 1) * step)
        partial = partial + through(gate_rest[span, :], up_rest[span, :], down_rest[span, :])
    halves_ref[0] = partial[:, :half]
    halves_ref[1] = partial[:, half:]
    keep_ref[...] = halves_ref[core]
    send_ref[...] = halves_ref[1 - core].astype(BF16)

    @pl.when(core == 0)
    def _():
        base_ref[...] = whole_ref[:, :half] + keep_ref[...]

    @pl.when(core == 1)
    def _():
        base_ref[...] = whole_ref[:, half:] + keep_ref[...]


def add_pair(keep_ref, got_ref, send_ref):
    send_ref[...] = (keep_ref[...] + got_ref[...].astype(F32)).astype(BF16)


def add_chips(base_ref, got_ref, first_ref, second_ref, third_ref, fetched_ref, out_ref):
    total = base_ref[...] + got_ref[...].astype(F32)
    total = total + first_ref[...].astype(F32) + second_ref[...].astype(F32) + third_ref[...].astype(F32)
    out_ref[...] = total.astype(BF16)


def fetch_half(place_ref, far_ref, out_ref, token_ref, copied):
    half = out_ref.shape[0]
    copy = pltpu.make_async_copy(
        far_ref.at[pl.ds(pl.multiple_of(place_ref[0] % 2 * half, 128), half)], out_ref, copied.at[0]
    )
    copy.start()
    token_ref[...] = jnp.zeros(token_ref.shape, F32)
    copy.wait()


def project_own(place_ref, own_ref, gain_ref, weight_ref, far_ref, acc_ref, square_ref, other_weight_ref, copied):
    half = own_ref.shape[1]
    core = place_ref[0] % 2
    near_rows = other_weight_ref.shape[0]
    copy = pltpu.make_async_copy(
        far_ref.at[pl.ds(pl.multiple_of((1 - core) * half, 128), near_rows)],
        other_weight_ref,
        copied.at[0],
    )
    copy.start()
    own = own_ref[...].astype(F32)
    square_ref[...] = jnp.broadcast_to(jnp.sum(own * own, axis=1, keepdims=True), square_ref.shape)
    scaled = (own * gain_ref[core]).astype(BF16)
    acc_ref[...] = jnp.dot(scaled, weight_ref[...], preferred_element_type=F32)
    copy.wait()


def project_other(
    place_ref,
    own_ref,
    other_ref,
    gain_ref,
    acc_ref,
    square_ref,
    front_ref,
    far_ref,
    shard_ref,
    out_ref,
    rest_ref,
    copied,
):
    half = own_ref.shape[1]
    core = place_ref[0] % 2
    near_rows = front_ref.shape[0]
    copy = pltpu.make_async_copy(
        far_ref.at[pl.ds(pl.multiple_of((1 - core) * half + near_rows, 128), half - near_rows)],
        rest_ref,
        copied.at[0],
    )
    copy.start()
    part = shard_ref.shape[1]
    parts = half // part
    for place in range(2 * parts):
        from_ref = own_ref if place // parts == place % 2 else other_ref
        column = place % parts * part

        @pl.when(place_ref[0] == place)
        def _():
            shard_ref[...] = from_ref[:, column : column + part]

    other = other_ref[...].astype(F32)
    square = square_ref[:, :1] + jnp.sum(other * other, axis=1, keepdims=True)
    scaled = (other * gain_ref[1 - core]).astype(BF16)
    acc = acc_ref[...] + jnp.dot(scaled[:, :near_rows], front_ref[...], preferred_element_type=F32)
    copy.wait()
    acc = acc + jnp.dot(scaled[:, near_rows:], rest_ref[...], preferred_element_type=F32)
    out_ref[...] = (acc * lax.rsqrt(square / (2 * half) + 1e-06)).astype(BF16)


SMEM = pl.BlockSpec(memory_space=pltpu.SMEM)
VMEM = pl.BlockSpec(memory_space=pltpu.VMEM)
FAR = pl.BlockSpec(memory_space=pl.ANY)


def near(array):
    return pltpu.with_memory_space_constraint(array, pltpu.VMEM)


def call(body, outs, scalars, arrays, far=(), scratch=(), copies=0, more=()):
    scratch_shapes = [pltpu.VMEM(shape, dtype) for shape, dtype in scratch] + list(more)
    if copies:
        scratch_shapes.append(pltpu.SemaphoreType.DMA((copies,)))
    return pl.pallas_call(
        body,
        out_shape=[
            pltpu.VMEM(shape, dtype) if stays else jax.ShapeDtypeStruct(shape, dtype)
            for shape, dtype, stays in outs
        ],
        in_specs=[SMEM] * len(scalars) + [VMEM] * len(arrays) + [FAR] * len(far),
        out_specs=[VMEM] * len(outs),
        scratch_shapes=scratch_shapes,
        name=body.__name__,
    )(*scalars, *[near(array) for array in arrays], *far)


def fetch(parts, after):
    def fetch_rows(*refs):
        fars, outs, copied = refs[1 : 1 + len(parts)], refs[1 + len(parts) : 1 + 2 * len(parts)], refs[-1]
        copies = [
            pltpu.make_async_copy(far.at[pl.ds(0, out.shape[0])], out, copied.at[index])
            for index, (far, out) in enumerate(zip(fars, outs))
        ]
        for copy in copies:
            copy.start()
        for copy in copies:
            copy.wait()

    return pl.pallas_call(
        fetch_rows,
        out_shape=[pltpu.VMEM((rows,) + far.shape[1:], far.dtype) for far, rows in parts]
        + [jax.ShapeDtypeStruct((8, 128), F32)],
        in_specs=[FAR] * (len(parts) + 1),
        out_specs=[VMEM] * (len(parts) + 1),
        scratch_shapes=[pltpu.SemaphoreType.DMA((len(parts),))],
        name="fetch_rows",
    )(after, *[far for far, _ in parts])


def exchange(copies, axis):
    return lax.all_to_all(copies, axis, split_axis=0, concat_axis=0, tiled=True)


def partner(block, distance):
    count = lax.axis_size("mlp")
    return lax.ppermute(block, "mlp", [(i, i ^ distance) for i in range(count)])


def gather(block):
    near = {0: block, **{distance: partner(block, distance) for distance in (2, 6, 4)}}
    far = {distance ^ 1: partner(near[distance], 1) for distance in near}
    return [{**near, **far}[distance] for distance in range(8)]


def shards(
    queries,
    new_kv,
    kv_cache,
    lengths,
    page_table,
    residual,
    out_weight,
    norm_gain,
    gate_weight,
    up_weight,
    down_weight,
    next_gain,
    qkv_weight,
):
    seq_count = lax.axis_size("seq")
    mlp_count = lax.axis_size("mlp")
    seq_place = lax.axis_index("seq")
    mlp_place = lax.axis_index("mlp")
    device = seq_place * mlp_count + mlp_place
    slot_count, page_len, kv_width = kv_cache.shape
    head_dim = kv_width // 2
    token_count, width = queries.shape
    page_count = page_table.shape[1]
    row_count, part_width = residual.shape
    half = width // 2

    query_rows = token_count * (width // head_dim)
    sent = pl.pallas_call(
        copy_queries,
        out_shape=jax.ShapeDtypeStruct((seq_count, token_count, width), BF16),
        in_specs=[VMEM],
        out_specs=VMEM,
        name="copy_queries",
    )(queries)
    arrived = exchange(sent, "seq")

    column_table = lax.dynamic_index_in_dim(
        page_table.reshape(seq_count, mlp_count, page_count), mlp_place, 1, keepdims=False
    )
    column_lengths = lax.dynamic_index_in_dim(
        lengths.reshape(seq_count, mlp_count), mlp_place, 1, keepdims=False
    )
    entry = (
        jnp.arange(seq_count, dtype=jnp.int32)[:, None] * page_count
        + jnp.arange(page_count, dtype=jnp.int32)[None, :]
        + 1
    )
    slots = device * slot_count + jnp.arange(slot_count, dtype=jnp.int32)
    codes = jnp.max(
        jnp.where(column_table[None] == slots[:, None, None], entry[None], 0), axis=(1, 2)
    )
    own_table = lax.dynamic_index_in_dim(column_table, seq_place, 0, keepdims=False)
    holder = (jnp.max(own_table) // (slot_count * mlp_count)).reshape(1)

    new_max, new_sum, new_acc = call(
        attend_new,
        [((token_count, 128), F32, True)] * 2 + [((token_count, width), F32, True)],
        [],
        [queries, new_kv],
    )
    near_slots = 11
    cache_front, _ = fetch([(kv_cache, near_slots)], sent)
    (held,) = call(
        attend_pages,
        [((seq_count, token_count, width + 128), BF16, False)],
        [codes, column_lengths],
        [arrived, cache_front],
        [kv_cache],
        [((slot_count, query_rows, page_len), F32)] * 2
        + [((slot_count, query_rows, head_dim), F32)]
        + [((slot_count - near_slots, page_len, kv_width), BF16)],
        1,
        [pltpu.SMEM((slot_count + 1,), jnp.int32)],
    )
    returned = exchange(held, "seq")
    attended, spread = call(
        merge_new,
        [((token_count, width), BF16, False), ((mlp_count, token_count, width), BF16, True)],
        [holder],
        [returned, new_max, new_sum, new_acc],
    )
    rows = exchange(spread, "mlp")
    layers = [(gate_weight.T, 96), (up_weight.T, 96), (down_weight, 96)]
    out_front, *front, _ = fetch([(out_weight.T, 128), *layers], held)
    (stream,) = call(
        project_out,
        [((row_count, part_width), BF16, True)],
        [],
        [rows, residual, out_front],
        [out_weight.T],
        [((part_width - 128, width), BF16)],
        1,
    )
    place = mlp_place.astype(jnp.int32).reshape(1)
    keep, send, base = call(
        feed_forward,
        [((row_count, half), F32, True), ((row_count, half), BF16, True), ((row_count, half), F32, True)],
        [place],
        [*gather(stream), norm_gain.reshape(1, width), *front],
        [far for far, _ in layers],
        [
            ((mlp_count, row_count, part_width), F32),
            ((row_count, width), F32),
            ((2, row_count, half), F32),
        ]
        + [((far.shape[0] - rows, width), BF16) for far, rows in layers],
        9,
    )
    got = partner(send, 1)
    (chip_half,) = call(add_pair, [((row_count, half), BF16, True)], [], [keep, got])
    others = [partner(chip_half, distance) for distance in (2, 6, 4)]
    columns = qkv_weight.shape[1]
    near_rows = 1152
    own_weight, fetched = pl.pallas_call(
        fetch_half,
        out_shape=[pltpu.VMEM((half, columns), BF16), jax.ShapeDtypeStruct((8, 128), F32)],
        in_specs=[SMEM, FAR],
        out_specs=[VMEM, VMEM],
        scratch_shapes=[pltpu.SemaphoreType.DMA((1,))],
        name="fetch_half",
    )(place, qkv_weight)
    (after_half,) = call(
        add_chips, [((row_count, half), BF16, True)], [], [base, got, *others], [fetched]
    )
    other_half = partner(after_half, 1)
    gains = next_gain.reshape(2, 1, half)
    acc, square, other_weight = call(
        project_own,
        [((row_count, columns), F32, True), ((row_count, 128), F32, True), ((near_rows, columns), BF16, True)],
        [place],
        [after_half, gains, own_weight],
        [qkv_weight],
        copies=1,
    )
    shard_after, next_qkv = call(
        project_other,
        [((row_count, part_width), BF16, False), ((row_count, columns), BF16, False)],
        [place],
        [after_half, other_half, gains, acc, square, other_weight],
        [qkv_weight],
        [((half - near_rows, columns), BF16)],
        1,
    )
    return (attended, shard_after, next_qkv)


def solution(mesh):
    return jax.shard_map(
        shards,
        mesh=mesh,
        in_specs=(
            P(("seq", "mlp"), None),
            P(("seq", "mlp"), None),
            P(("seq", "mlp"), None, None),
            P(),
            P(),
            P("seq", "mlp"),
            P(None, "mlp"),
            P(),
            P(None, "mlp"),
            P(None, "mlp"),
            P("mlp", None),
            P(),
            P(None, "mlp"),
        ),
        out_specs=(P(("seq", "mlp"), None), P("seq", "mlp"), P("seq", "mlp")),
        check_vma=False,
    )
```

```python
import jax
import jax.numpy as jnp
from jax import lax
from jax.experimental import pallas as pl
from jax.experimental.pallas import tpu as pltpu
from jax.sharding import PartitionSpec as P

WINDOW = 2048
NEG_FILL = -1e30
LAST = (((1,), (1,)), ((), ()))
F32 = jnp.float32
BF16 = jnp.bfloat16


def head_major(values, head_dim):
    width = values.shape[1]
    return jnp.concatenate(
        [values[:, start : start + head_dim] for start in range(0, width, head_dim)], axis=0
    )


def put_heads(column, token_count, lanes):
    lane = lax.broadcasted_iota(jnp.int32, (token_count, lanes), 1)
    placed = jnp.zeros((token_count, lanes), F32)
    for head in range(column.shape[0] // token_count):
        part = column[head * token_count : (head + 1) * token_count, :]
        placed = jnp.where(lane == head, part, placed)
    return placed


def copy_queries(queries_ref, out_ref):
    queries = queries_ref[...]
    for place in range(out_ref.shape[0]):
        out_ref[place] = queries


def attend_new(queries_ref, new_ref, max_ref, sum_ref, acc_ref):
    token_count, width = queries_ref.shape
    head_dim = new_ref.shape[1] // 2
    query = head_major(queries_ref[...].astype(F32), head_dim).astype(BF16)
    scores = lax.dot_general(
        query, new_ref[:, :head_dim], LAST, preferred_element_type=F32
    ) * head_dim ** (-0.5)
    token = lax.broadcasted_iota(jnp.int32, scores.shape, 0) % token_count
    column = lax.broadcasted_iota(jnp.int32, scores.shape, 1)
    valid = column <= token
    peak = jnp.max(jnp.where(valid, scores, NEG_FILL), axis=1, keepdims=True)
    weights = jnp.where(valid, jnp.exp(scores - peak), 0.0)
    rounded = weights.astype(BF16).astype(F32)
    values = new_ref[:, head_dim:].astype(F32)
    acc = jnp.zeros((query.shape[0], head_dim), F32)
    for new in range(token_count):
        acc = acc + rounded[:, new : new + 1] * values[new : new + 1, :]
    max_ref[...] = put_heads(peak, token_count, max_ref.shape[1])
    sum_ref[...] = put_heads(jnp.sum(weights, axis=1, keepdims=True), token_count, sum_ref.shape[1])
    for head in range(width // head_dim):
        acc_ref[:, head * head_dim : (head + 1) * head_dim] = acc[
            head * token_count : (head + 1) * token_count, :
        ]


def attend_pages(
    code_ref, length_ref, rows_ref, front_ref, far_ref, out_ref, score_ref, peak_ref, acc_ref, rest_ref, end_ref, copied
):
    slot_count, page_len, kv_width = far_ref.shape
    near_count = front_ref.shape[0]
    rest = pltpu.make_async_copy(
        far_ref.at[pl.ds(near_count, slot_count - near_count)], rest_ref, copied.at[0]
    )
    rest.start()

    def cached(slot, span):
        if slot < near_count:
            return front_ref[slot, :, span]
        return rest_ref[slot - near_count, :, span]

    head_dim = kv_width // 2
    token_count = out_ref.shape[1]
    width = out_ref.shape[2] - 128
    query_rows = token_count * (width // head_dim)
    head_count = width // head_dim
    page_count = 128
    scale = head_dim ** (-0.5)
    token = lax.broadcasted_iota(jnp.int32, (query_rows, page_len), 0) % token_count
    lane = lax.broadcasted_iota(jnp.int32, (query_rows, page_len), 1)
    low_edge = lane - token + (WINDOW - 1)
    codes = [code_ref[slot] for slot in range(slot_count)]
    sources = [jnp.maximum(code - 1, 0) // page_count for code in codes]
    first = [True] + [
        (codes[slot] == 0) | (codes[slot - 1] == 0) | (sources[slot] != sources[slot - 1])
        for slot in range(1, slot_count)
    ]
    last = first[1:] + [True]
    fill = jnp.full((query_rows, page_len), NEG_FILL, F32)
    peak = fill
    for slot in range(slot_count):
        if slot == near_count:
            rest.wait()
        page = jnp.maximum(codes[slot] - 1, 0) % page_count
        reach = jnp.where(codes[slot] > 0, length_ref[sources[slot]], 0) - page * page_len
        scores = (
            lax.dot_general(
                head_major(rows_ref[sources[slot]].astype(F32), head_dim).astype(BF16),
                cached(slot, slice(0, head_dim)),
                LAST, preferred_element_type=F32
            )
            * scale
        )
        scores = jnp.where((lane < reach) & (low_edge >= reach), scores, NEG_FILL)
        score_ref[slot] = scores
        peak = jnp.maximum(scores, jnp.where(first[slot], NEG_FILL, peak) if slot else fill)
        peak_ref[slot] = jnp.broadcast_to(jnp.max(peak, axis=1, keepdims=True), (query_rows, page_len))
    peak = peak_ref[slot_count - 1]
    for slot in range(slot_count - 2, -1, -1):
        peak = jnp.where(last[slot], peak_ref[slot], peak)
        peak_ref[slot] = peak
    total = jnp.zeros((query_rows, page_len), F32)
    acc = jnp.zeros((query_rows, head_dim), F32)
    held = jnp.int32(0)
    for slot in range(slot_count):
        weights = jnp.exp(score_ref[slot] - peak_ref[slot])
        value = jnp.dot(
            weights.astype(BF16), cached(slot, slice(head_dim, kv_width)), preferred_element_type=F32
        )
        total = weights + (jnp.where(first[slot], 0.0, total) if slot else 0.0)
        acc = value + (jnp.where(first[slot], 0.0, acc) if slot else 0.0)
        score_ref[slot] = total
        acc_ref[slot] = acc
        end_ref[held] = slot
        held = held + ((codes[slot] > 0) & last[slot]).astype(jnp.int32)
    lanes = lax.broadcasted_iota(jnp.int32, (token_count, 128), 1)
    for turn in range(slot_count // 2):
        slot = end_ref[jnp.where(turn < held, turn, 0)]
        source = jnp.maximum(code_ref[slot] - 1, 0) // page_count
        whole_sum = jnp.sum(score_ref[slot], axis=1, keepdims=True)
        result = acc_ref[slot] / whole_sum
        for head in range(head_count):
            out_ref[source, :, head * head_dim : (head + 1) * head_dim] = result[
                head * token_count : (head + 1) * token_count, :
            ].astype(BF16)
        whole = put_heads(peak_ref[slot][:, :1] + jnp.log(whole_sum), token_count, 128)
        high = whole.astype(BF16).astype(F32)
        middle = (whole - high).astype(BF16).astype(F32)
        low = whole - high - middle
        packed = jnp.where(
            lanes < 16, high, jnp.where(lanes < 32, pltpu.roll(middle, 16, 1), pltpu.roll(low, 32, 1))
        )
        out_ref[source, :, width:] = packed.astype(BF16)


def merge_new(holder_ref, got_ref, max_ref, sum_ref, acc_ref, attended_ref, spread_ref):
    holder = holder_ref[0]
    head_dim = 256
    width = attended_ref.shape[1]
    packed = got_ref[holder, :, width:].astype(F32)
    cached = packed + pltpu.roll(packed, 128 - 16, 1) + pltpu.roll(packed, 128 - 32, 1)
    new_max = max_ref[...]
    peak = jnp.maximum(cached, new_max)
    cached_factor = jnp.exp(cached - peak)
    new_factor = jnp.exp(new_max - peak)
    inverse = 1.0 / (cached_factor + new_factor * sum_ref[...])
    cached_factor = cached_factor * inverse
    new_factor = new_factor * inverse
    for head in range(width // head_dim):
        span = slice(head * head_dim, (head + 1) * head_dim)
        rows = (
            got_ref[holder, :, span].astype(F32) * cached_factor[:, head : head + 1]
            + acc_ref[:, span] * new_factor[:, head : head + 1]
        ).astype(BF16)
        attended_ref[:, span] = rows
        for place in range(spread_ref.shape[0]):
            spread_ref[place, :, span] = rows


def project_out(rows_ref, residual_ref, weight_ref, out_ref):
    places = rows_ref.shape[0]
    rows = jnp.concatenate([rows_ref[place].astype(F32) for place in range(places)], axis=0).astype(BF16)
    attention_out = lax.dot_general(rows, weight_ref[...], LAST, preferred_element_type=F32)
    out_ref[...] = (residual_ref[...].astype(F32) + attention_out).astype(BF16)


def stack_blocks(first_ref, second_ref, third_ref, fourth_ref, fetched_ref, out_ref):
    for index, block_ref in enumerate((first_ref, second_ref, third_ref, fourth_ref)):
        out_ref[index] = block_ref[...]


def feed_forward(place_ref, *refs):
    mine_ref, theirs_ref, gain_ref, gate_ref, up_ref, down_ref, gate_far, up_far, down_far = refs[:9]
    keep_ref, send_ref, stream_half_ref = refs[9:12]
    stream_ref, whole_ref, halves_ref, gate_rest, up_rest, down_rest, copied = refs[12:]
    parts, rows, width = stream_ref.shape
    total = parts * width
    half = total // 2
    near_rows = gate_ref.shape[0]
    chunks = copied.shape[0] // 3
    step = gate_rest.shape[0] // chunks
    copies = []
    for chunk in range(chunks):
        for far, rest in ((gate_far, gate_rest), (up_far, up_rest), (down_far, down_rest)):
            copies.append(
                pltpu.make_async_copy(
                    far.at[pl.ds(near_rows + chunk * step, step)],
                    rest.at[pl.ds(chunk * step, step)],
                    copied.at[len(copies)],
                )
            )
            copies[-1].start()
    for index, distance in enumerate(DISTANCES):
        stream_ref[place_ref[0] ^ distance] = mine_ref[index].astype(F32)
        stream_ref[place_ref[0] ^ distance ^ 1] = theirs_ref[index].astype(F32)
    for part in range(parts):
        whole_ref[:, part * width : (part + 1) * width] = stream_ref[part]
    whole = whole_ref[...]
    square = jnp.sum(whole * whole, axis=1, keepdims=True)
    normed = (whole * lax.rsqrt(square / total + 1e-06) * gain_ref[...]).astype(BF16)
    core = place_ref[0] % 2

    @pl.when(core == 0)
    def _():
        stream_half_ref[...] = whole_ref[:, :half].astype(BF16)

    @pl.when(core == 1)
    def _():
        stream_half_ref[...] = whole_ref[:, half:].astype(BF16)

    def through(gate_rows, up_rows, down_rows):
        gate = lax.dot_general(normed, gate_rows, LAST, preferred_element_type=F32)
        upward = lax.dot_general(normed, up_rows, LAST, preferred_element_type=F32)
        hidden = (jax.nn.gelu(gate, approximate=True) * upward).astype(BF16)
        return jnp.dot(hidden, down_rows, preferred_element_type=F32)

    partial = through(gate_ref[...], up_ref[...], down_ref[...])
    for chunk in range(chunks):
        for copy in copies[3 * chunk : 3 * chunk + 3]:
            copy.wait()
        span = slice(chunk * step, (chunk + 1) * step)
        partial = partial + through(gate_rest[span, :], up_rest[span, :], down_rest[span, :])
    halves_ref[0] = partial[:, :half]
    halves_ref[1] = partial[:, half:]
    keep_ref[...] = halves_ref[core]
    send_ref[...] = halves_ref[1 - core].astype(BF16)


def add_pair(keep_ref, got_ref, send_ref):
    send_ref[...] = (keep_ref[...] + got_ref[...].astype(F32)).astype(BF16)


def add_chips(keep_ref, got_ref, first_ref, second_ref, third_ref, stream_ref, fetched_ref, out_ref):
    total = keep_ref[...] + got_ref[...].astype(F32)
    total = total + first_ref[...].astype(F32) + second_ref[...].astype(F32) + third_ref[...].astype(F32)
    out_ref[...] = (stream_ref[...].astype(F32) + total).astype(BF16)


def fetch_half(place_ref, far_ref, out_ref, token_ref, copied):
    half = far_ref.shape[0] // 2
    copy = pltpu.make_async_copy(
        far_ref.at[pl.ds(pl.multiple_of(place_ref[0] % 2 * half, 128), out_ref.shape[0])],
        out_ref,
        copied.at[0],
    )
    copy.start()
    token_ref[...] = jnp.zeros(token_ref.shape, F32)
    copy.wait()


def project_own(
    place_ref,
    own_ref,
    gain_ref,
    front_ref,
    far_ref,
    acc_ref,
    square_ref,
    other_weight_ref,
    rest_ref,
    copied,
):
    half = own_ref.shape[1]
    core = place_ref[0] % 2
    near_rows = other_weight_ref.shape[0]
    copy = pltpu.make_async_copy(
        far_ref.at[pl.ds(pl.multiple_of((1 - core) * half, 128), near_rows)],
        other_weight_ref,
        copied.at[0],
    )
    own_rows = front_ref.shape[0]
    rest = pltpu.make_async_copy(
        far_ref.at[pl.ds(pl.multiple_of(core * half + own_rows, 128), half - own_rows)],
        rest_ref,
        copied.at[1],
    )
    rest.start()
    copy.start()
    own = own_ref[...].astype(F32)
    square_ref[...] = jnp.broadcast_to(jnp.sum(own * own, axis=1, keepdims=True), square_ref.shape)
    scaled = (own * gain_ref[core]).astype(BF16)
    acc = jnp.dot(scaled[:, :own_rows], front_ref[...], preferred_element_type=F32)
    rest.wait()
    acc_ref[...] = acc + jnp.dot(scaled[:, own_rows:], rest_ref[...], preferred_element_type=F32)
    copy.wait()


def project_other(
    place_ref,
    own_ref,
    other_ref,
    gain_ref,
    acc_ref,
    square_ref,
    front_ref,
    far_ref,
    shard_ref,
    out_ref,
    rest_ref,
    copied,
):
    half = own_ref.shape[1]
    core = place_ref[0] % 2
    near_rows = front_ref.shape[0]
    copy = pltpu.make_async_copy(
        far_ref.at[pl.ds(pl.multiple_of((1 - core) * half + near_rows, 128), half - near_rows)],
        rest_ref,
        copied.at[0],
    )
    copy.start()
    part = shard_ref.shape[1]
    parts = half // part
    for place in range(2 * parts):
        from_ref = own_ref if place // parts == place % 2 else other_ref
        column = place % parts * part

        @pl.when(place_ref[0] == place)
        def _():
            shard_ref[...] = from_ref[:, column : column + part]

    other = other_ref[...].astype(F32)
    square = square_ref[:, :1] + jnp.sum(other * other, axis=1, keepdims=True)
    scaled = (other * gain_ref[1 - core]).astype(BF16)
    acc = acc_ref[...] + jnp.dot(scaled[:, :near_rows], front_ref[...], preferred_element_type=F32)
    copy.wait()
    acc = acc + jnp.dot(scaled[:, near_rows:], rest_ref[...], preferred_element_type=F32)
    out_ref[...] = (acc * lax.rsqrt(square / (2 * half) + 1e-06)).astype(BF16)


SMEM = pl.BlockSpec(memory_space=pltpu.SMEM)
VMEM = pl.BlockSpec(memory_space=pltpu.VMEM)
FAR = pl.BlockSpec(memory_space=pl.ANY)
DISTANCES = (0, 2, 6, 4)
NEAR = 128


def near(array):
    return pltpu.with_memory_space_constraint(array, pltpu.VMEM)


def call(body, outs, scalars, arrays, far=(), scratch=(), copies=0, more=()):
    scratch_shapes = [pltpu.VMEM(shape, dtype) for shape, dtype in scratch] + list(more)
    if copies:
        scratch_shapes.append(pltpu.SemaphoreType.DMA((copies,)))
    return pl.pallas_call(
        body,
        out_shape=[
            pltpu.VMEM(shape, dtype) if stays else jax.ShapeDtypeStruct(shape, dtype)
            for shape, dtype, stays in outs
        ],
        in_specs=[SMEM] * len(scalars) + [VMEM] * len(arrays) + [FAR] * len(far),
        out_specs=[VMEM] * len(outs),
        scratch_shapes=scratch_shapes,
        name=body.__name__,
    )(*scalars, *[near(array) for array in arrays], *far)


def fetch(parts, after):
    def fetch_rows(*refs):
        fars, outs, copied = refs[1 : 1 + len(parts)], refs[1 + len(parts) : 1 + 2 * len(parts)], refs[-1]
        copies = [
            pltpu.make_async_copy(far.at[pl.ds(0, out.shape[0])], out, copied.at[index])
            for index, (far, out) in enumerate(zip(fars, outs))
        ]
        for copy in copies:
            copy.start()
        for copy in copies:
            copy.wait()

    return pl.pallas_call(
        fetch_rows,
        out_shape=[pltpu.VMEM((rows,) + far.shape[1:], far.dtype) for far, rows in parts]
        + [jax.ShapeDtypeStruct((8, 128), F32)],
        in_specs=[FAR] * (len(parts) + 1),
        out_specs=[VMEM] * (len(parts) + 1),
        scratch_shapes=[pltpu.SemaphoreType.DMA((len(parts),))],
        name="fetch_rows",
    )(after, *[far for far, _ in parts])


def exchange(copies, axis):
    return lax.all_to_all(copies, axis, split_axis=0, concat_axis=0, tiled=True)


def partner(block, distance):
    count = lax.axis_size("mlp")
    return lax.ppermute(block, "mlp", [(i, i ^ distance) for i in range(count)])


def shards(
    queries,
    new_kv,
    kv_cache,
    lengths,
    page_table,
    residual,
    out_weight,
    norm_gain,
    gate_weight,
    up_weight,
    down_weight,
    next_gain,
    qkv_weight,
):
    seq_count = lax.axis_size("seq")
    mlp_count = lax.axis_size("mlp")
    seq_place = lax.axis_index("seq")
    mlp_place = lax.axis_index("mlp")
    device = seq_place * mlp_count + mlp_place
    slot_count, page_len, kv_width = kv_cache.shape
    head_dim = kv_width // 2
    token_count, width = queries.shape
    page_count = page_table.shape[1]
    row_count, part_width = residual.shape
    half = width // 2

    query_rows = token_count * (width // head_dim)
    sent = pl.pallas_call(
        copy_queries,
        out_shape=jax.ShapeDtypeStruct((seq_count, token_count, width), BF16),
        in_specs=[VMEM],
        out_specs=VMEM,
        name="copy_queries",
    )(queries)
    arrived = exchange(sent, "seq")

    column_table = lax.dynamic_index_in_dim(
        page_table.reshape(seq_count, mlp_count, page_count), mlp_place, 1, keepdims=False
    )
    column_lengths = lax.dynamic_index_in_dim(
        lengths.reshape(seq_count, mlp_count), mlp_place, 1, keepdims=False
    )
    entry = (
        jnp.arange(seq_count, dtype=jnp.int32)[:, None] * page_count
        + jnp.arange(page_count, dtype=jnp.int32)[None, :]
        + 1
    )
    slots = device * slot_count + jnp.arange(slot_count, dtype=jnp.int32)
    codes = jnp.max(
        jnp.where(column_table[None] == slots[:, None, None], entry[None], 0), axis=(1, 2)
    )
    own_table = lax.dynamic_index_in_dim(column_table, seq_place, 0, keepdims=False)
    holder = (jnp.max(own_table) // (slot_count * mlp_count)).reshape(1)

    new_max, new_sum, new_acc = call(
        attend_new,
        [((token_count, 128), F32, True)] * 2 + [((token_count, width), F32, True)],
        [],
        [queries, new_kv],
    )
    near_slots = 11
    cache_front, _ = fetch([(kv_cache, near_slots)], sent)
    (held,) = call(
        attend_pages,
        [((seq_count, token_count, width + 128), BF16, False)],
        [codes, column_lengths],
        [arrived, cache_front],
        [kv_cache],
        [((slot_count, query_rows, page_len), F32)] * 2
        + [((slot_count, query_rows, head_dim), F32)]
        + [((slot_count - near_slots, page_len, kv_width), BF16)],
        1,
        [pltpu.SMEM((slot_count + 1,), jnp.int32)],
    )
    returned = exchange(held, "seq")
    attended, spread = call(
        merge_new,
        [((token_count, width), BF16, False), ((mlp_count, token_count, width), BF16, True)],
        [holder],
        [returned, new_max, new_sum, new_acc],
    )
    rows = exchange(spread, "mlp")
    out_near, _ = fetch([(out_weight.T, part_width)], held)
    (stream,) = call(
        project_out,
        [((row_count, part_width), BF16, True)],
        [],
        [rows, residual, out_near],
    )
    layers = [(gate_weight.T, NEAR), (up_weight.T, NEAR), (down_weight, NEAR)]
    *front, fetched = fetch(layers, held)
    (mine,) = call(
        stack_blocks,
        [((4, row_count, part_width), BF16, True)],
        [],
        [stream, *[partner(stream, distance) for distance in DISTANCES[1:]]],
        [fetched],
    )
    theirs = partner(mine, 1)
    place = mlp_place.astype(jnp.int32).reshape(1)
    keep, send, stream_half = call(
        feed_forward,
        [((row_count, half), F32, True), ((row_count, half), BF16, True), ((row_count, half), BF16, True)],
        [place],
        [mine, theirs, norm_gain.reshape(1, width), *front],
        [far for far, _ in layers],
        [
            ((mlp_count, row_count, part_width), F32),
            ((row_count, width), F32),
            ((2, row_count, half), F32),
        ]
        + [((far.shape[0] - rows, width), BF16) for far, rows in layers],
        6,
    )
    got = partner(send, 1)
    (chip_half,) = call(add_pair, [((row_count, half), BF16, True)], [], [keep, got])
    others = [partner(chip_half, distance) for distance in DISTANCES[1:]]
    columns = qkv_weight.shape[1]
    own_rows = 1152
    near_rows = 1152
    own_weight, fetched = pl.pallas_call(
        fetch_half,
        out_shape=[pltpu.VMEM((own_rows, columns), BF16), jax.ShapeDtypeStruct((8, 128), F32)],
        in_specs=[SMEM, FAR],
        out_specs=[VMEM, VMEM],
        scratch_shapes=[pltpu.SemaphoreType.DMA((1,))],
        name="fetch_half",
    )(place, qkv_weight)
    (after_half,) = call(
        add_chips, [((row_count, half), BF16, True)], [], [keep, got, *others, stream_half], [fetched]
    )
    other_half = partner(after_half, 1)
    gains = next_gain.reshape(2, 1, half)
    acc, square, other_weight = call(
        project_own,
        [((row_count, columns), F32, True), ((row_count, 128), F32, True), ((near_rows, columns), BF16, True)],
        [place],
        [after_half, gains, own_weight],
        [qkv_weight],
        [((half - own_rows, columns), BF16)],
        2,
    )
    shard_after, next_qkv = call(
        project_other,
        [((row_count, part_width), BF16, False), ((row_count, columns), BF16, False)],
        [place],
        [after_half, other_half, gains, acc, square, other_weight],
        [qkv_weight],
        [((half - near_rows, columns), BF16)],
        1,
    )
    return (attended, shard_after, next_qkv)


def solution(mesh):
    return jax.shard_map(
        shards,
        mesh=mesh,
        in_specs=(
            P(("seq", "mlp"), None),
            P(("seq", "mlp"), None),
            P(("seq", "mlp"), None, None),
            P(),
            P(),
            P("seq", "mlp"),
            P(None, "mlp"),
            P(),
            P(None, "mlp"),
            P(None, "mlp"),
            P("mlp", None),
            P(),
            P(None, "mlp"),
        ),
        out_specs=(P(("seq", "mlp"), None), P("seq", "mlp"), P("seq", "mlp")),
        check_vma=False,
    )
```

```python
import jax
import jax.numpy as jnp
from jax import lax
from jax.experimental import pallas as pl
from jax.experimental.pallas import tpu as pltpu
from jax.sharding import PartitionSpec as P

WINDOW = 2048
NEG_FILL = -1e30
LAST = (((1,), (1,)), ((), ()))
F32 = jnp.float32
BF16 = jnp.bfloat16


def head_major(values, head_dim):
    width = values.shape[1]
    return jnp.concatenate(
        [values[:, start : start + head_dim] for start in range(0, width, head_dim)], axis=0
    )


def put_heads(column, token_count, lanes):
    lane = lax.broadcasted_iota(jnp.int32, (token_count, lanes), 1)
    placed = jnp.zeros((token_count, lanes), F32)
    for head in range(column.shape[0] // token_count):
        part = column[head * token_count : (head + 1) * token_count, :]
        placed = jnp.where(lane == head, part, placed)
    return placed


def copy_queries(queries_ref, out_ref):
    queries = queries_ref[...]
    for place in range(out_ref.shape[0]):
        out_ref[place] = queries


def attend_new(queries_ref, new_ref, max_ref, sum_ref, acc_ref):
    token_count, width = queries_ref.shape
    head_dim = new_ref.shape[1] // 2
    query = head_major(queries_ref[...].astype(F32), head_dim).astype(BF16)
    scores = lax.dot_general(
        query, new_ref[:, :head_dim], LAST, preferred_element_type=F32
    ) * head_dim ** (-0.5)
    token = lax.broadcasted_iota(jnp.int32, scores.shape, 0) % token_count
    column = lax.broadcasted_iota(jnp.int32, scores.shape, 1)
    valid = column <= token
    peak = jnp.max(jnp.where(valid, scores, NEG_FILL), axis=1, keepdims=True)
    weights = jnp.where(valid, jnp.exp(scores - peak), 0.0)
    rounded = weights.astype(BF16).astype(F32)
    values = new_ref[:, head_dim:].astype(F32)
    acc = jnp.zeros((query.shape[0], head_dim), F32)
    for new in range(token_count):
        acc = acc + rounded[:, new : new + 1] * values[new : new + 1, :]
    max_ref[...] = put_heads(peak, token_count, max_ref.shape[1])
    sum_ref[...] = put_heads(jnp.sum(weights, axis=1, keepdims=True), token_count, sum_ref.shape[1])
    for head in range(width // head_dim):
        acc_ref[:, head * head_dim : (head + 1) * head_dim] = acc[
            head * token_count : (head + 1) * token_count, :
        ]


def attend_pages(
    code_ref, length_ref, rows_ref, front_ref, far_ref, out_ref, score_ref, peak_ref, acc_ref, rest_ref, end_ref, copied
):
    slot_count, page_len, kv_width = far_ref.shape
    near_count = front_ref.shape[0]
    rest = pltpu.make_async_copy(
        far_ref.at[pl.ds(near_count, slot_count - near_count)], rest_ref, copied.at[0]
    )
    rest.start()

    def cached(slot, span):
        if slot < near_count:
            return front_ref[slot, :, span]
        return rest_ref[slot - near_count, :, span]

    head_dim = kv_width // 2
    token_count = out_ref.shape[1]
    width = out_ref.shape[2] - 128
    query_rows = token_count * (width // head_dim)
    head_count = width // head_dim
    page_count = 128
    scale = head_dim ** (-0.5)
    token = lax.broadcasted_iota(jnp.int32, (query_rows, page_len), 0) % token_count
    lane = lax.broadcasted_iota(jnp.int32, (query_rows, page_len), 1)
    low_edge = lane - token + (WINDOW - 1)
    codes = [code_ref[slot] for slot in range(slot_count)]
    sources = [jnp.maximum(code - 1, 0) // page_count for code in codes]
    first = [True] + [
        (codes[slot] == 0) | (codes[slot - 1] == 0) | (sources[slot] != sources[slot - 1])
        for slot in range(1, slot_count)
    ]
    last = first[1:] + [True]
    fill = jnp.full((query_rows, page_len), NEG_FILL, F32)
    peak = fill
    for slot in range(slot_count):
        if slot == near_count:
            rest.wait()
        page = jnp.maximum(codes[slot] - 1, 0) % page_count
        reach = jnp.where(codes[slot] > 0, length_ref[sources[slot]], 0) - page * page_len
        scores = (
            lax.dot_general(
                head_major(rows_ref[sources[slot]].astype(F32), head_dim).astype(BF16),
                cached(slot, slice(0, head_dim)),
                LAST, preferred_element_type=F32
            )
            * scale
        )
        scores = jnp.where((lane < reach) & (low_edge >= reach), scores, NEG_FILL)
        score_ref[slot] = scores
        peak = jnp.maximum(scores, jnp.where(first[slot], NEG_FILL, peak) if slot else fill)
        peak_ref[slot] = jnp.broadcast_to(jnp.max(peak, axis=1, keepdims=True), (query_rows, page_len))
    peak = peak_ref[slot_count - 1]
    for slot in range(slot_count - 2, -1, -1):
        peak = jnp.where(last[slot], peak_ref[slot], peak)
        peak_ref[slot] = peak
    total = jnp.zeros((query_rows, page_len), F32)
    acc = jnp.zeros((query_rows, head_dim), F32)
    held = jnp.int32(0)
    for slot in range(slot_count):
        weights = jnp.exp(score_ref[slot] - peak_ref[slot])
        value = jnp.dot(
            weights.astype(BF16), cached(slot, slice(head_dim, kv_width)), preferred_element_type=F32
        )
        total = weights + (jnp.where(first[slot], 0.0, total) if slot else 0.0)
        acc = value + (jnp.where(first[slot], 0.0, acc) if slot else 0.0)
        score_ref[slot] = total
        acc_ref[slot] = acc
        end_ref[held] = slot
        held = held + ((codes[slot] > 0) & last[slot]).astype(jnp.int32)
    lanes = lax.broadcasted_iota(jnp.int32, (token_count, 128), 1)
    for turn in range(slot_count // 2):
        slot = end_ref[jnp.where(turn < held, turn, 0)]
        source = jnp.maximum(code_ref[slot] - 1, 0) // page_count
        whole_sum = jnp.sum(score_ref[slot], axis=1, keepdims=True)
        result = acc_ref[slot] / whole_sum
        for head in range(head_count):
            out_ref[source, :, head * head_dim : (head + 1) * head_dim] = result[
                head * token_count : (head + 1) * token_count, :
            ].astype(BF16)
        whole = put_heads(peak_ref[slot][:, :1] + jnp.log(whole_sum), token_count, 128)
        high = whole.astype(BF16).astype(F32)
        middle = (whole - high).astype(BF16).astype(F32)
        low = whole - high - middle
        packed = jnp.where(
            lanes < 16, high, jnp.where(lanes < 32, pltpu.roll(middle, 16, 1), pltpu.roll(low, 32, 1))
        )
        out_ref[source, :, width:] = packed.astype(BF16)


def merge_new(holder_ref, got_ref, max_ref, sum_ref, acc_ref, attended_ref):
    holder = holder_ref[0]
    head_dim = 256
    width = attended_ref.shape[1]
    packed = got_ref[holder, :, width:].astype(F32)
    cached = packed + pltpu.roll(packed, 128 - 16, 1) + pltpu.roll(packed, 128 - 32, 1)
    new_max = max_ref[...]
    peak = jnp.maximum(cached, new_max)
    cached_factor = jnp.exp(cached - peak)
    new_factor = jnp.exp(new_max - peak)
    inverse = 1.0 / (cached_factor + new_factor * sum_ref[...])
    cached_factor = cached_factor * inverse
    new_factor = new_factor * inverse
    for head in range(width // head_dim):
        span = slice(head * head_dim, (head + 1) * head_dim)
        rows = (
            got_ref[holder, :, span].astype(F32) * cached_factor[:, head : head + 1]
            + acc_ref[:, span] * new_factor[:, head : head + 1]
        ).astype(BF16)
        attended_ref[:, span] = rows


def project_out(place_ref, mine_ref, theirs_ref, residual_ref, *refs):
    weight_refs, out_ref, rows_ref = refs[:-2], refs[-2], refs[-1]
    for index, distance in enumerate(DISTANCES):
        rows_ref[place_ref[0] ^ distance] = mine_ref[index].astype(F32)
        rows_ref[place_ref[0] ^ distance ^ 1] = theirs_ref[index].astype(F32)
    rows = jnp.concatenate([rows_ref[place] for place in range(rows_ref.shape[0])], axis=0).astype(BF16)
    start = 0
    for weight_ref in weight_refs:
        span = slice(start, start + weight_ref.shape[0])
        attention_out = lax.dot_general(rows, weight_ref[...], LAST, preferred_element_type=F32)
        out_ref[:, span] = (residual_ref[:, span].astype(F32) + attention_out).astype(BF16)
        start += weight_ref.shape[0]


def stack_blocks(first_ref, second_ref, third_ref, fourth_ref, fetched_ref, out_ref):
    for index, block_ref in enumerate((first_ref, second_ref, third_ref, fourth_ref)):
        out_ref[index] = block_ref[...]


def feed_forward(place_ref, *refs):
    mine_ref, theirs_ref, gain_ref, gate_ref, up_ref, down_ref, gate_far, up_far, down_far = refs[:9]
    keep_ref, send_ref, stream_half_ref = refs[9:12]
    stream_ref, whole_ref, halves_ref, gate_rest, up_rest, down_rest, copied = refs[12:]
    parts, rows, width = stream_ref.shape
    total = parts * width
    half = total // 2
    near_rows = gate_ref.shape[0]
    chunks = copied.shape[0] // 3
    step = gate_rest.shape[0] // chunks
    copies = []
    for chunk in range(chunks):
        for far, rest in ((gate_far, gate_rest), (up_far, up_rest), (down_far, down_rest)):
            copies.append(
                pltpu.make_async_copy(
                    far.at[pl.ds(near_rows + chunk * step, step)],
                    rest.at[pl.ds(chunk * step, step)],
                    copied.at[len(copies)],
                )
            )
            copies[-1].start()
    for index, distance in enumerate(DISTANCES):
        stream_ref[place_ref[0] ^ distance] = mine_ref[index].astype(F32)
        stream_ref[place_ref[0] ^ distance ^ 1] = theirs_ref[index].astype(F32)
    for part in range(parts):
        whole_ref[:, part * width : (part + 1) * width] = stream_ref[part]
    whole = whole_ref[...]
    square = jnp.sum(whole * whole, axis=1, keepdims=True)
    normed = (whole * lax.rsqrt(square / total + 1e-06) * gain_ref[...]).astype(BF16)
    core = place_ref[0] % 2

    @pl.when(core == 0)
    def _():
        stream_half_ref[...] = whole_ref[:, :half].astype(BF16)

    @pl.when(core == 1)
    def _():
        stream_half_ref[...] = whole_ref[:, half:].astype(BF16)

    def through(gate_rows, up_rows, down_rows):
        gate = lax.dot_general(normed, gate_rows, LAST, preferred_element_type=F32)
        upward = lax.dot_general(normed, up_rows, LAST, preferred_element_type=F32)
        hidden = (jax.nn.gelu(gate, approximate=True) * upward).astype(BF16)
        return jnp.dot(hidden, down_rows, preferred_element_type=F32)

    partial = through(gate_ref[...], up_ref[...], down_ref[...])
    for chunk in range(chunks):
        for copy in copies[3 * chunk : 3 * chunk + 3]:
            copy.wait()
        span = slice(chunk * step, (chunk + 1) * step)
        partial = partial + through(gate_rest[span, :], up_rest[span, :], down_rest[span, :])
    halves_ref[0] = partial[:, :half]
    halves_ref[1] = partial[:, half:]
    keep_ref[...] = halves_ref[core]
    send_ref[...] = halves_ref[1 - core].astype(BF16)


def add_pair(keep_ref, got_ref, send_ref):
    send_ref[...] = (keep_ref[...] + got_ref[...].astype(F32)).astype(BF16)


def add_chips(keep_ref, got_ref, first_ref, second_ref, third_ref, stream_ref, fetched_ref, out_ref):
    total = keep_ref[...] + got_ref[...].astype(F32)
    total = total + first_ref[...].astype(F32) + second_ref[...].astype(F32) + third_ref[...].astype(F32)
    out_ref[...] = (stream_ref[...].astype(F32) + total).astype(BF16)


def fetch_half(place_ref, far_ref, out_ref, token_ref, copied):
    half = far_ref.shape[0] // 2
    copy = pltpu.make_async_copy(
        far_ref.at[pl.ds(pl.multiple_of(place_ref[0] % 2 * half, 128), out_ref.shape[0])],
        out_ref,
        copied.at[0],
    )
    copy.start()
    token_ref[...] = jnp.zeros(token_ref.shape, F32)
    copy.wait()


def project_own(
    place_ref,
    own_ref,
    gain_ref,
    front_ref,
    far_ref,
    acc_ref,
    square_ref,
    other_weight_ref,
    rest_ref,
    copied,
):
    half = own_ref.shape[1]
    core = place_ref[0] % 2
    near_rows = other_weight_ref.shape[0]
    copy = pltpu.make_async_copy(
        far_ref.at[pl.ds(pl.multiple_of((1 - core) * half, 128), near_rows)],
        other_weight_ref,
        copied.at[0],
    )
    own_rows = front_ref.shape[0]
    rest = pltpu.make_async_copy(
        far_ref.at[pl.ds(pl.multiple_of(core * half + own_rows, 128), half - own_rows)],
        rest_ref,
        copied.at[1],
    )
    rest.start()
    copy.start()
    own = own_ref[...].astype(F32)
    square_ref[...] = jnp.broadcast_to(jnp.sum(own * own, axis=1, keepdims=True), square_ref.shape)
    scaled = (own * gain_ref[core]).astype(BF16)
    acc = jnp.dot(scaled[:, :own_rows], front_ref[...], preferred_element_type=F32)
    rest.wait()
    acc_ref[...] = acc + jnp.dot(scaled[:, own_rows:], rest_ref[...], preferred_element_type=F32)
    copy.wait()


def project_other(
    place_ref,
    own_ref,
    other_ref,
    gain_ref,
    acc_ref,
    square_ref,
    front_ref,
    far_ref,
    shard_ref,
    out_ref,
    rest_ref,
    copied,
):
    half = own_ref.shape[1]
    core = place_ref[0] % 2
    near_rows = front_ref.shape[0]
    copy = pltpu.make_async_copy(
        far_ref.at[pl.ds(pl.multiple_of((1 - core) * half + near_rows, 128), half - near_rows)],
        rest_ref,
        copied.at[0],
    )
    copy.start()
    part = shard_ref.shape[1]
    parts = half // part
    for place in range(2 * parts):
        from_ref = own_ref if place // parts == place % 2 else other_ref
        column = place % parts * part

        @pl.when(place_ref[0] == place)
        def _():
            shard_ref[...] = from_ref[:, column : column + part]

    other = other_ref[...].astype(F32)
    square = square_ref[:, :1] + jnp.sum(other * other, axis=1, keepdims=True)
    scaled = (other * gain_ref[1 - core]).astype(BF16)
    acc = acc_ref[...] + jnp.dot(scaled[:, :near_rows], front_ref[...], preferred_element_type=F32)
    copy.wait()
    acc = acc + jnp.dot(scaled[:, near_rows:], rest_ref[...], preferred_element_type=F32)
    out_ref[...] = (acc * lax.rsqrt(square / (2 * half) + 1e-06)).astype(BF16)


SMEM = pl.BlockSpec(memory_space=pltpu.SMEM)
VMEM = pl.BlockSpec(memory_space=pltpu.VMEM)
FAR = pl.BlockSpec(memory_space=pl.ANY)
DISTANCES = (0, 2, 6, 4)
NEAR = 128


def near(array):
    return pltpu.with_memory_space_constraint(array, pltpu.VMEM)


def call(body, outs, scalars, arrays, far=(), scratch=(), copies=0, more=()):
    scratch_shapes = [pltpu.VMEM(shape, dtype) for shape, dtype in scratch] + list(more)
    if copies:
        scratch_shapes.append(pltpu.SemaphoreType.DMA((copies,)))
    return pl.pallas_call(
        body,
        out_shape=[
            pltpu.VMEM(shape, dtype) if stays else jax.ShapeDtypeStruct(shape, dtype)
            for shape, dtype, stays in outs
        ],
        in_specs=[SMEM] * len(scalars) + [VMEM] * len(arrays) + [FAR] * len(far),
        out_specs=[VMEM] * len(outs),
        scratch_shapes=scratch_shapes,
        name=body.__name__,
    )(*scalars, *[near(array) for array in arrays], *far)


def fetch(parts, after, carried=None):
    extra = [] if carried is None else [carried]
    count = len(parts)

    def fetch_rows(*refs):
        fars, refs = refs[1 : 1 + count], refs[1 + count :]
        if extra:
            refs[1 + count + 1][...] = refs[0][...]
            refs = refs[1:]
        copies = [
            pltpu.make_async_copy(far.at[pl.ds(start, rows)], out, refs[-1].at[index])
            for index, (far, out, (_, rows, start)) in enumerate(zip(fars, refs, parts))
        ]
        for copy in copies:
            copy.start()
        for copy in copies:
            copy.wait()

    return pl.pallas_call(
        fetch_rows,
        out_shape=[pltpu.VMEM((rows,) + far.shape[1:], far.dtype) for far, rows, _ in parts]
        + [jax.ShapeDtypeStruct((8, 128), F32)]
        + [jax.ShapeDtypeStruct(array.shape, array.dtype) for array in extra],
        in_specs=[FAR] * (count + 1) + [VMEM] * len(extra),
        out_specs=[VMEM] * (count + 1 + len(extra)),
        scratch_shapes=[pltpu.SemaphoreType.DMA((count,))],
        name="fetch_rows",
    )(after, *[far for far, _, _ in parts], *[near(array) for array in extra])


def exchange(copies, axis):
    return lax.all_to_all(copies, axis, split_axis=0, concat_axis=0, tiled=True)


def partner(block, distance):
    count = lax.axis_size("mlp")
    return lax.ppermute(block, "mlp", [(i, i ^ distance) for i in range(count)])


def gather(block, fetched):
    others = [partner(block, distance) for distance in DISTANCES[1:]]
    (mine,) = call(
        stack_blocks, [((4,) + block.shape, BF16, True)], [], [block, *others], [fetched]
    )
    return mine, partner(mine, 1)


def shards(
    queries,
    new_kv,
    kv_cache,
    lengths,
    page_table,
    residual,
    out_weight,
    norm_gain,
    gate_weight,
    up_weight,
    down_weight,
    next_gain,
    qkv_weight,
):
    seq_count = lax.axis_size("seq")
    mlp_count = lax.axis_size("mlp")
    seq_place = lax.axis_index("seq")
    mlp_place = lax.axis_index("mlp")
    device = seq_place * mlp_count + mlp_place
    slot_count, page_len, kv_width = kv_cache.shape
    head_dim = kv_width // 2
    token_count, width = queries.shape
    page_count = page_table.shape[1]
    row_count, part_width = residual.shape
    half = width // 2

    query_rows = token_count * (width // head_dim)
    sent = pl.pallas_call(
        copy_queries,
        out_shape=jax.ShapeDtypeStruct((seq_count, token_count, width), BF16),
        in_specs=[VMEM],
        out_specs=VMEM,
        name="copy_queries",
    )(queries)
    arrived = exchange(sent, "seq")

    column_table = lax.dynamic_index_in_dim(
        page_table.reshape(seq_count, mlp_count, page_count), mlp_place, 1, keepdims=False
    )
    column_lengths = lax.dynamic_index_in_dim(
        lengths.reshape(seq_count, mlp_count), mlp_place, 1, keepdims=False
    )
    entry = (
        jnp.arange(seq_count, dtype=jnp.int32)[:, None] * page_count
        + jnp.arange(page_count, dtype=jnp.int32)[None, :]
        + 1
    )
    slots = device * slot_count + jnp.arange(slot_count, dtype=jnp.int32)
    codes = jnp.max(
        jnp.where(column_table[None] == slots[:, None, None], entry[None], 0), axis=(1, 2)
    )
    own_table = lax.dynamic_index_in_dim(column_table, seq_place, 0, keepdims=False)
    holder = (jnp.max(own_table) // (slot_count * mlp_count)).reshape(1)

    new_max, new_sum, new_acc = call(
        attend_new,
        [((token_count, 128), F32, True)] * 2 + [((token_count, width), F32, True)],
        [],
        [queries, new_kv],
    )
    near_slots = 11
    cache_front, _ = fetch([(kv_cache, near_slots, 0)], sent)
    (held,) = call(
        attend_pages,
        [((seq_count, token_count, width + 128), BF16, False)],
        [codes, column_lengths],
        [arrived, cache_front],
        [kv_cache],
        [((slot_count, query_rows, page_len), F32)] * 2
        + [((slot_count, query_rows, head_dim), F32)]
        + [((slot_count - near_slots, page_len, kv_width), BF16)],
        1,
        [pltpu.SMEM((slot_count + 1,), jnp.int32)],
    )
    returned = exchange(held, "seq")
    (attended,) = call(
        merge_new,
        [((token_count, width), BF16, True)],
        [holder],
        [returned, new_max, new_sum, new_acc],
    )
    place = mlp_place.astype(jnp.int32).reshape(1)
    spans = [(128, 0), (128, 128), (64, 256)]
    *out_near, fetched = fetch([(out_weight.T, rows, start) for rows, start in spans], held)
    mine, theirs = gather(attended, fetched)
    (stream,) = call(
        project_out,
        [((row_count, part_width), BF16, True)],
        [place],
        [mine, theirs, residual, *out_near],
        scratch=[((mlp_count, token_count, width), F32)],
    )
    layers = [(gate_weight.T, NEAR), (up_weight.T, NEAR), (down_weight, NEAR)]
    *front, fetched, attended_out = fetch([(far, rows, 0) for far, rows in layers], held, attended)
    mine, theirs = gather(stream, fetched)
    keep, send, stream_half = call(
        feed_forward,
        [((row_count, half), F32, True), ((row_count, half), BF16, True), ((row_count, half), BF16, True)],
        [place],
        [mine, theirs, norm_gain.reshape(1, width), *front],
        [far for far, _ in layers],
        [
            ((mlp_count, row_count, part_width), F32),
            ((row_count, width), F32),
            ((2, row_count, half), F32),
        ]
        + [((far.shape[0] - rows, width), BF16) for far, rows in layers],
        6,
    )
    got = partner(send, 1)
    (chip_half,) = call(add_pair, [((row_count, half), BF16, True)], [], [keep, got])
    others = [partner(chip_half, distance) for distance in DISTANCES[1:]]
    columns = qkv_weight.shape[1]
    own_rows = 1152
    near_rows = 1152
    own_weight, fetched = pl.pallas_call(
        fetch_half,
        out_shape=[pltpu.VMEM((own_rows, columns), BF16), jax.ShapeDtypeStruct((8, 128), F32)],
        in_specs=[SMEM, FAR],
        out_specs=[VMEM, VMEM],
        scratch_shapes=[pltpu.SemaphoreType.DMA((1,))],
        name="fetch_half",
    )(place, qkv_weight)
    (after_half,) = call(
        add_chips, [((row_count, half), BF16, True)], [], [keep, got, *others, stream_half], [fetched]
    )
    other_half = partner(after_half, 1)
    gains = next_gain.reshape(2, 1, half)
    acc, square, other_weight = call(
        project_own,
        [((row_count, columns), F32, True), ((row_count, 128), F32, True), ((near_rows, columns), BF16, True)],
        [place],
        [after_half, gains, own_weight],
        [qkv_weight],
        [((half - own_rows, columns), BF16)],
        2,
    )
    shard_after, next_qkv = call(
        project_other,
        [((row_count, part_width), BF16, False), ((row_count, columns), BF16, False)],
        [place],
        [after_half, other_half, gains, acc, square, other_weight],
        [qkv_weight],
        [((half - near_rows, columns), BF16)],
        1,
    )
    return (attended_out, shard_after, next_qkv)


def solution(mesh):
    return jax.shard_map(
        shards,
        mesh=mesh,
        in_specs=(
            P(("seq", "mlp"), None),
            P(("seq", "mlp"), None),
            P(("seq", "mlp"), None, None),
            P(),
            P(),
            P("seq", "mlp"),
            P(None, "mlp"),
            P(),
            P(None, "mlp"),
            P(None, "mlp"),
            P("mlp", None),
            P(),
            P(None, "mlp"),
        ),
        out_specs=(P(("seq", "mlp"), None), P("seq", "mlp"), P("seq", "mlp")),
        check_vma=False,
    )
```

```python
import jax
import jax.numpy as jnp
from jax import lax
from jax.experimental import pallas as pl
from jax.experimental.pallas import tpu as pltpu
from jax.sharding import PartitionSpec as P

WINDOW = 2048
NEG_FILL = -1e30
LAST = (((1,), (1,)), ((), ()))
F32 = jnp.float32
BF16 = jnp.bfloat16


def head_major(values, head_dim):
    width = values.shape[1]
    return jnp.concatenate(
        [values[:, start : start + head_dim] for start in range(0, width, head_dim)], axis=0
    )


def put_heads(column, token_count, lanes):
    lane = lax.broadcasted_iota(jnp.int32, (token_count, lanes), 1)
    placed = jnp.zeros((token_count, lanes), F32)
    for head in range(column.shape[0] // token_count):
        part = column[head * token_count : (head + 1) * token_count, :]
        placed = jnp.where(lane == head, part, placed)
    return placed


def copy_queries(queries_ref, out_ref):
    queries = queries_ref[...]
    for place in range(out_ref.shape[0]):
        out_ref[place] = queries


def attend_new(queries_ref, new_ref, max_ref, sum_ref, acc_ref):
    token_count, width = queries_ref.shape
    head_dim = new_ref.shape[1] // 2
    query = head_major(queries_ref[...].astype(F32), head_dim).astype(BF16)
    scores = lax.dot_general(
        query, new_ref[:, :head_dim], LAST, preferred_element_type=F32
    ) * head_dim ** (-0.5)
    token = lax.broadcasted_iota(jnp.int32, scores.shape, 0) % token_count
    column = lax.broadcasted_iota(jnp.int32, scores.shape, 1)
    valid = column <= token
    peak = jnp.max(jnp.where(valid, scores, NEG_FILL), axis=1, keepdims=True)
    weights = jnp.where(valid, jnp.exp(scores - peak), 0.0)
    rounded = weights.astype(BF16).astype(F32)
    values = new_ref[:, head_dim:].astype(F32)
    acc = jnp.zeros((query.shape[0], head_dim), F32)
    for new in range(token_count):
        acc = acc + rounded[:, new : new + 1] * values[new : new + 1, :]
    max_ref[...] = put_heads(peak, token_count, max_ref.shape[1])
    sum_ref[...] = put_heads(jnp.sum(weights, axis=1, keepdims=True), token_count, sum_ref.shape[1])
    for head in range(width // head_dim):
        acc_ref[:, head * head_dim : (head + 1) * head_dim] = acc[
            head * token_count : (head + 1) * token_count, :
        ]


def attend_pages(
    code_ref, length_ref, rows_ref, front_ref, far_ref, out_ref, score_ref, peak_ref, acc_ref, rest_ref, end_ref, copied
):
    slot_count, page_len, kv_width = far_ref.shape
    near_count = front_ref.shape[0]
    rest = pltpu.make_async_copy(
        far_ref.at[pl.ds(near_count, slot_count - near_count)], rest_ref, copied.at[0]
    )
    rest.start()

    def cached(slot, span):
        if slot < near_count:
            return front_ref[slot, :, span]
        return rest_ref[slot - near_count, :, span]

    head_dim = kv_width // 2
    token_count = out_ref.shape[1]
    width = out_ref.shape[2] - 128
    query_rows = token_count * (width // head_dim)
    head_count = width // head_dim
    page_count = 128
    scale = head_dim ** (-0.5)
    token = lax.broadcasted_iota(jnp.int32, (query_rows, page_len), 0) % token_count
    lane = lax.broadcasted_iota(jnp.int32, (query_rows, page_len), 1)
    low_edge = lane - token + (WINDOW - 1)
    codes = [code_ref[slot] for slot in range(slot_count)]
    sources = [jnp.maximum(code - 1, 0) // page_count for code in codes]
    first = [True] + [
        (codes[slot] == 0) | (codes[slot - 1] == 0) | (sources[slot] != sources[slot - 1])
        for slot in range(1, slot_count)
    ]
    last = first[1:] + [True]
    fill = jnp.full((query_rows, page_len), NEG_FILL, F32)
    peak = fill
    for slot in range(slot_count):
        if slot == near_count:
            rest.wait()
        page = jnp.maximum(codes[slot] - 1, 0) % page_count
        reach = jnp.where(codes[slot] > 0, length_ref[sources[slot]], 0) - page * page_len
        scores = (
            lax.dot_general(
                head_major(rows_ref[sources[slot]].astype(F32), head_dim).astype(BF16),
                cached(slot, slice(0, head_dim)),
                LAST, preferred_element_type=F32
            )
            * scale
        )
        scores = jnp.where((lane < reach) & (low_edge >= reach), scores, NEG_FILL)
        score_ref[slot] = scores
        peak = jnp.maximum(scores, jnp.where(first[slot], NEG_FILL, peak) if slot else fill)
        peak_ref[slot] = jnp.broadcast_to(jnp.max(peak, axis=1, keepdims=True), (query_rows, page_len))
    peak = peak_ref[slot_count - 1]
    for slot in range(slot_count - 2, -1, -1):
        peak = jnp.where(last[slot], peak_ref[slot], peak)
        peak_ref[slot] = peak
    total = jnp.zeros((query_rows, page_len), F32)
    acc = jnp.zeros((query_rows, head_dim), F32)
    held = jnp.int32(0)
    for slot in range(slot_count):
        weights = jnp.exp(score_ref[slot] - peak_ref[slot])
        value = jnp.dot(
            weights.astype(BF16), cached(slot, slice(head_dim, kv_width)), preferred_element_type=F32
        )
        total = weights + (jnp.where(first[slot], 0.0, total) if slot else 0.0)
        acc = value + (jnp.where(first[slot], 0.0, acc) if slot else 0.0)
        score_ref[slot] = total
        acc_ref[slot] = acc
        end_ref[held] = slot
        held = held + ((codes[slot] > 0) & last[slot]).astype(jnp.int32)
    lanes = lax.broadcasted_iota(jnp.int32, (token_count, 128), 1)
    for turn in range(slot_count // 2):
        slot = end_ref[jnp.where(turn < held, turn, 0)]
        source = jnp.maximum(code_ref[slot] - 1, 0) // page_count
        whole_sum = jnp.sum(score_ref[slot], axis=1, keepdims=True)
        result = acc_ref[slot] / whole_sum
        for head in range(head_count):
            out_ref[source, :, head * head_dim : (head + 1) * head_dim] = result[
                head * token_count : (head + 1) * token_count, :
            ].astype(BF16)
        whole = put_heads(peak_ref[slot][:, :1] + jnp.log(whole_sum), token_count, 128)
        high = whole.astype(BF16).astype(F32)
        middle = (whole - high).astype(BF16).astype(F32)
        low = whole - high - middle
        packed = jnp.where(
            lanes < 16, high, jnp.where(lanes < 32, pltpu.roll(middle, 16, 1), pltpu.roll(low, 32, 1))
        )
        out_ref[source, :, width:] = packed.astype(BF16)


def merge_new(holder_ref, got_ref, max_ref, sum_ref, acc_ref, attended_ref):
    holder = holder_ref[0]
    head_dim = 256
    width = attended_ref.shape[1]
    packed = got_ref[holder, :, width:].astype(F32)
    cached = packed + pltpu.roll(packed, 128 - 16, 1) + pltpu.roll(packed, 128 - 32, 1)
    new_max = max_ref[...]
    peak = jnp.maximum(cached, new_max)
    cached_factor = jnp.exp(cached - peak)
    new_factor = jnp.exp(new_max - peak)
    inverse = 1.0 / (cached_factor + new_factor * sum_ref[...])
    cached_factor = cached_factor * inverse
    new_factor = new_factor * inverse
    for head in range(width // head_dim):
        span = slice(head * head_dim, (head + 1) * head_dim)
        rows = (
            got_ref[holder, :, span].astype(F32) * cached_factor[:, head : head + 1]
            + acc_ref[:, span] * new_factor[:, head : head + 1]
        ).astype(BF16)
        attended_ref[:, span] = rows


def project_out(place_ref, mine_ref, theirs_ref, residual_ref, *refs):
    weight_refs, out_ref, rows_ref = refs[:-2], refs[-2], refs[-1]
    for index, distance in enumerate(DISTANCES):
        rows_ref[place_ref[0] ^ distance] = mine_ref[index].astype(F32)
        rows_ref[place_ref[0] ^ distance ^ 1] = theirs_ref[index].astype(F32)
    rows = jnp.concatenate([rows_ref[place] for place in range(rows_ref.shape[0])], axis=0).astype(BF16)
    start = 0
    for weight_ref in weight_refs:
        span = slice(start, start + weight_ref.shape[0])
        attention_out = lax.dot_general(rows, weight_ref[...], LAST, preferred_element_type=F32)
        out_ref[:, span] = (residual_ref[:, span].astype(F32) + attention_out).astype(BF16)
        start += weight_ref.shape[0]


def stack_blocks(first_ref, second_ref, third_ref, fourth_ref, fetched_ref, out_ref):
    for index, block_ref in enumerate((first_ref, second_ref, third_ref, fourth_ref)):
        out_ref[index] = block_ref[...]


def feed_forward(place_ref, *refs):
    mine_ref, theirs_ref, gain_ref, gate_ref, up_ref, down_ref, gate_far, up_far, down_far = refs[:9]
    keep_ref, send_ref, stream_half_ref = refs[9:12]
    stream_ref, whole_ref, halves_ref, gate_rest, up_rest, down_rest, copied = refs[12:]
    parts, rows, width = stream_ref.shape
    total = parts * width
    half = total // 2
    near_rows = gate_ref.shape[0]
    chunks = copied.shape[0] // 3
    step = gate_rest.shape[0] // chunks
    copies = []
    for chunk in range(chunks):
        for far, rest in ((gate_far, gate_rest), (up_far, up_rest), (down_far, down_rest)):
            copies.append(
                pltpu.make_async_copy(
                    far.at[pl.ds(near_rows + chunk * step, step)],
                    rest.at[pl.ds(chunk * step, step)],
                    copied.at[len(copies)],
                )
            )
            copies[-1].start()
    for index, distance in enumerate(DISTANCES):
        stream_ref[place_ref[0] ^ distance] = mine_ref[index].astype(F32)
        stream_ref[place_ref[0] ^ distance ^ 1] = theirs_ref[index].astype(F32)
    for part in range(parts):
        whole_ref[:, part * width : (part + 1) * width] = stream_ref[part]
    whole = whole_ref[...]
    square = jnp.sum(whole * whole, axis=1, keepdims=True)
    normed = (whole * lax.rsqrt(square / total + 1e-06) * gain_ref[...]).astype(BF16)
    core = place_ref[0] % 2

    @pl.when(core == 0)
    def _():
        stream_half_ref[...] = whole_ref[:, :half].astype(BF16)

    @pl.when(core == 1)
    def _():
        stream_half_ref[...] = whole_ref[:, half:].astype(BF16)

    def through(gate_rows, up_rows, down_rows):
        gate = lax.dot_general(normed, gate_rows, LAST, preferred_element_type=F32)
        upward = lax.dot_general(normed, up_rows, LAST, preferred_element_type=F32)
        hidden = (jax.nn.gelu(gate, approximate=True) * upward).astype(BF16)
        return jnp.dot(hidden, down_rows, preferred_element_type=F32)

    partial = through(gate_ref[...], up_ref[...], down_ref[...])
    for chunk in range(chunks):
        for copy in copies[3 * chunk : 3 * chunk + 3]:
            copy.wait()
        span = slice(chunk * step, (chunk + 1) * step)
        partial = partial + through(gate_rest[span, :], up_rest[span, :], down_rest[span, :])
    halves_ref[0] = partial[:, :half]
    halves_ref[1] = partial[:, half:]
    keep_ref[...] = halves_ref[core]
    send_ref[...] = halves_ref[1 - core].astype(BF16)


def add_pair(keep_ref, got_ref, send_ref):
    send_ref[...] = (keep_ref[...] + got_ref[...].astype(F32)).astype(BF16)


def add_chips(keep_ref, got_ref, first_ref, second_ref, third_ref, stream_ref, fetched_ref, out_ref):
    total = keep_ref[...] + got_ref[...].astype(F32)
    total = total + first_ref[...].astype(F32) + second_ref[...].astype(F32) + third_ref[...].astype(F32)
    out_ref[...] = (stream_ref[...].astype(F32) + total).astype(BF16)


def fetch_half(place_ref, far_ref, out_ref, token_ref, copied):
    half = far_ref.shape[0] // 2
    copy = pltpu.make_async_copy(
        far_ref.at[pl.ds(pl.multiple_of(place_ref[0] % 2 * half, 128), out_ref.shape[0])],
        out_ref,
        copied.at[0],
    )
    copy.start()
    token_ref[...] = jnp.zeros(token_ref.shape, F32)
    copy.wait()


def project_own(
    place_ref,
    own_ref,
    gain_ref,
    front_ref,
    far_ref,
    acc_ref,
    square_ref,
    first_ref,
    second_ref,
    rest_ref,
    copied,
):
    half = own_ref.shape[1]
    core = place_ref[0] % 2
    quarter = half // 2
    copies = [
        pltpu.make_async_copy(
            far_ref.at[pl.ds(pl.multiple_of((1 - core) * half + index * quarter, 128), quarter)],
            ref,
            copied.at[index],
        )
        for index, ref in enumerate((first_ref, second_ref))
    ]
    own_rows = front_ref.shape[0]
    rest = pltpu.make_async_copy(
        far_ref.at[pl.ds(pl.multiple_of(core * half + own_rows, 128), half - own_rows)],
        rest_ref,
        copied.at[2],
    )
    rest.start()
    for copy in copies:
        copy.start()
    own = own_ref[...].astype(F32)
    square_ref[...] = jnp.broadcast_to(jnp.sum(own * own, axis=1, keepdims=True), square_ref.shape)
    scaled = (own * gain_ref[core]).astype(BF16)
    acc = jnp.dot(scaled[:, :own_rows], front_ref[...], preferred_element_type=F32)
    rest.wait()
    acc_ref[...] = acc + jnp.dot(scaled[:, own_rows:], rest_ref[...], preferred_element_type=F32)
    for copy in copies:
        copy.wait()


def project_other(
    place_ref,
    own_ref,
    other_ref,
    gain_ref,
    acc_ref,
    square_ref,
    first_ref,
    second_ref,
    shard_ref,
    out_ref,
):
    half = own_ref.shape[1]
    core = place_ref[0] % 2
    quarter = half // 2
    part = shard_ref.shape[1]
    parts = half // part
    for place in range(2 * parts):
        from_ref = own_ref if place // parts == place % 2 else other_ref
        column = place % parts * part

        @pl.when(place_ref[0] == place)
        def _():
            shard_ref[...] = from_ref[:, column : column + part]

    other = other_ref[...].astype(F32)
    square = square_ref[:, :1] + jnp.sum(other * other, axis=1, keepdims=True)
    scaled = (other * gain_ref[1 - core]).astype(BF16)
    acc = acc_ref[...] + jnp.dot(scaled[:, :quarter], first_ref[...], preferred_element_type=F32)
    acc = acc + jnp.dot(scaled[:, quarter:], second_ref[...], preferred_element_type=F32)
    out_ref[...] = (acc * lax.rsqrt(square / (2 * half) + 1e-06)).astype(BF16)


SMEM = pl.BlockSpec(memory_space=pltpu.SMEM)
VMEM = pl.BlockSpec(memory_space=pltpu.VMEM)
FAR = pl.BlockSpec(memory_space=pl.ANY)
DISTANCES = (0, 2, 6, 4)
NEAR = 128


def near(array):
    return pltpu.with_memory_space_constraint(array, pltpu.VMEM)


def call(body, outs, scalars, arrays, far=(), scratch=(), copies=0, more=()):
    scratch_shapes = [pltpu.VMEM(shape, dtype) for shape, dtype in scratch] + list(more)
    if copies:
        scratch_shapes.append(pltpu.SemaphoreType.DMA((copies,)))
    return pl.pallas_call(
        body,
        out_shape=[
            pltpu.VMEM(shape, dtype) if stays else jax.ShapeDtypeStruct(shape, dtype)
            for shape, dtype, stays in outs
        ],
        in_specs=[SMEM] * len(scalars) + [VMEM] * len(arrays) + [FAR] * len(far),
        out_specs=[VMEM] * len(outs),
        scratch_shapes=scratch_shapes,
        name=body.__name__,
    )(*scalars, *[near(array) for array in arrays], *far)


def fetch(parts, after, carried=None):
    extra = [] if carried is None else [carried]
    count = len(parts)

    def fetch_rows(*refs):
        fars, refs = refs[1 : 1 + count], refs[1 + count :]
        if extra:
            refs[1 + count + 1][...] = refs[0][...]
            refs = refs[1:]
        copies = [
            pltpu.make_async_copy(far.at[pl.ds(start, rows)], out, refs[-1].at[index])
            for index, (far, out, (_, rows, start)) in enumerate(zip(fars, refs, parts))
        ]
        for copy in copies:
            copy.start()
        for copy in copies:
            copy.wait()

    return pl.pallas_call(
        fetch_rows,
        out_shape=[pltpu.VMEM((rows,) + far.shape[1:], far.dtype) for far, rows, _ in parts]
        + [jax.ShapeDtypeStruct((8, 128), F32)]
        + [jax.ShapeDtypeStruct(array.shape, array.dtype) for array in extra],
        in_specs=[FAR] * (count + 1) + [VMEM] * len(extra),
        out_specs=[VMEM] * (count + 1 + len(extra)),
        scratch_shapes=[pltpu.SemaphoreType.DMA((count,))],
        name="fetch_rows",
    )(after, *[far for far, _, _ in parts], *[near(array) for array in extra])


def exchange(copies, axis):
    return lax.all_to_all(copies, axis, split_axis=0, concat_axis=0, tiled=True)


def partner(block, distance):
    count = lax.axis_size("mlp")
    return lax.ppermute(block, "mlp", [(i, i ^ distance) for i in range(count)])


def gather(block, fetched):
    others = [partner(block, distance) for distance in DISTANCES[1:]]
    (mine,) = call(
        stack_blocks, [((4,) + block.shape, BF16, True)], [], [block, *others], [fetched]
    )
    return mine, partner(mine, 1)


def shards(
    queries,
    new_kv,
    kv_cache,
    lengths,
    page_table,
    residual,
    out_weight,
    norm_gain,
    gate_weight,
    up_weight,
    down_weight,
    next_gain,
    qkv_weight,
):
    seq_count = lax.axis_size("seq")
    mlp_count = lax.axis_size("mlp")
    seq_place = lax.axis_index("seq")
    mlp_place = lax.axis_index("mlp")
    device = seq_place * mlp_count + mlp_place
    slot_count, page_len, kv_width = kv_cache.shape
    head_dim = kv_width // 2
    token_count, width = queries.shape
    page_count = page_table.shape[1]
    row_count, part_width = residual.shape
    half = width // 2

    query_rows = token_count * (width // head_dim)
    sent = pl.pallas_call(
        copy_queries,
        out_shape=jax.ShapeDtypeStruct((seq_count, token_count, width), BF16),
        in_specs=[VMEM],
        out_specs=VMEM,
        name="copy_queries",
    )(queries)
    arrived = exchange(sent, "seq")

    column_table = lax.dynamic_index_in_dim(
        page_table.reshape(seq_count, mlp_count, page_count), mlp_place, 1, keepdims=False
    )
    column_lengths = lax.dynamic_index_in_dim(
        lengths.reshape(seq_count, mlp_count), mlp_place, 1, keepdims=False
    )
    entry = (
        jnp.arange(seq_count, dtype=jnp.int32)[:, None] * page_count
        + jnp.arange(page_count, dtype=jnp.int32)[None, :]
        + 1
    )
    slots = device * slot_count + jnp.arange(slot_count, dtype=jnp.int32)
    codes = jnp.max(
        jnp.where(column_table[None] == slots[:, None, None], entry[None], 0), axis=(1, 2)
    )
    own_table = lax.dynamic_index_in_dim(column_table, seq_place, 0, keepdims=False)
    holder = (jnp.max(own_table) // (slot_count * mlp_count)).reshape(1)

    new_max, new_sum, new_acc = call(
        attend_new,
        [((token_count, 128), F32, True)] * 2 + [((token_count, width), F32, True)],
        [],
        [queries, new_kv],
    )
    near_slots = 11
    cache_front, _ = fetch([(kv_cache, near_slots, 0)], sent)
    (held,) = call(
        attend_pages,
        [((seq_count, token_count, width + 128), BF16, False)],
        [codes, column_lengths],
        [arrived, cache_front],
        [kv_cache],
        [((slot_count, query_rows, page_len), F32)] * 2
        + [((slot_count, query_rows, head_dim), F32)]
        + [((slot_count - near_slots, page_len, kv_width), BF16)],
        1,
        [pltpu.SMEM((slot_count + 1,), jnp.int32)],
    )
    returned = exchange(held, "seq")
    (attended,) = call(
        merge_new,
        [((token_count, width), BF16, True)],
        [holder],
        [returned, new_max, new_sum, new_acc],
    )
    place = mlp_place.astype(jnp.int32).reshape(1)
    spans = [(128, 0), (128, 128), (64, 256)]
    *out_near, fetched = fetch([(out_weight.T, rows, start) for rows, start in spans], held)
    mine, theirs = gather(attended, fetched)
    (stream,) = call(
        project_out,
        [((row_count, part_width), BF16, True)],
        [place],
        [mine, theirs, residual, *out_near],
        scratch=[((mlp_count, token_count, width), F32)],
    )
    layers = [(gate_weight.T, NEAR), (up_weight.T, NEAR), (down_weight, NEAR)]
    *front, fetched, attended_out = fetch([(far, rows, 0) for far, rows in layers], held, attended)
    mine, theirs = gather(stream, fetched)
    keep, send, stream_half = call(
        feed_forward,
        [((row_count, half), F32, True), ((row_count, half), BF16, True), ((row_count, half), BF16, True)],
        [place],
        [mine, theirs, norm_gain.reshape(1, width), *front],
        [far for far, _ in layers],
        [
            ((mlp_count, row_count, part_width), F32),
            ((row_count, width), F32),
            ((2, row_count, half), F32),
        ]
        + [((far.shape[0] - rows, width), BF16) for far, rows in layers],
        6,
    )
    got = partner(send, 1)
    (chip_half,) = call(add_pair, [((row_count, half), BF16, True)], [], [keep, got])
    others = [partner(chip_half, distance) for distance in DISTANCES[1:]]
    columns = qkv_weight.shape[1]
    own_rows = 1152
    own_weight, fetched = pl.pallas_call(
        fetch_half,
        out_shape=[pltpu.VMEM((own_rows, columns), BF16), jax.ShapeDtypeStruct((8, 128), F32)],
        in_specs=[SMEM, FAR],
        out_specs=[VMEM, VMEM],
        scratch_shapes=[pltpu.SemaphoreType.DMA((1,))],
        name="fetch_half",
    )(place, qkv_weight)
    (after_half,) = call(
        add_chips, [((row_count, half), BF16, True)], [], [keep, got, *others, stream_half], [fetched]
    )
    other_half = partner(after_half, 1)
    gains = next_gain.reshape(2, 1, half)
    acc, square, *other_weights = call(
        project_own,
        [((row_count, columns), F32, True), ((row_count, 128), F32, True)]
        + [((half // 2, columns), BF16, True)] * 2,
        [place],
        [after_half, gains, own_weight],
        [qkv_weight],
        [((half - own_rows, columns), BF16)],
        3,
    )
    shard_after, next_qkv = call(
        project_other,
        [((row_count, part_width), BF16, False), ((row_count, columns), BF16, False)],
        [place],
        [after_half, other_half, gains, acc, square, *other_weights],
    )
    return (attended_out, shard_after, next_qkv)


def solution(mesh):
    return jax.shard_map(
        shards,
        mesh=mesh,
        in_specs=(
            P(("seq", "mlp"), None),
            P(("seq", "mlp"), None),
            P(("seq", "mlp"), None, None),
            P(),
            P(),
            P("seq", "mlp"),
            P(None, "mlp"),
            P(),
            P(None, "mlp"),
            P(None, "mlp"),
            P("mlp", None),
            P(),
            P(None, "mlp"),
        ),
        out_specs=(P(("seq", "mlp"), None), P("seq", "mlp"), P("seq", "mlp")),
        check_vma=False,
    )
```
